128 devices in a mesh: prow: 4 (over x), pcol: 32 (over y, z, core).
Axes of the slice: x: 4, y: 4, z: 4, core: 2. Of those that a mesh axis runs over, the one named last changes fastest.
Arguments:
- matrix: float32 [128, 4, 128, 1, 32, 128], P(None, 'prow', None, None, 'pcol')
- pivots: int32 [128], replicated, may hold values from 0 to 65535, as said below
Outputs:
- factored: float32 [128, 4, 128, 1, 32, 128], P(None, 'prow', None, None, 'pcol')
The draws below stay inside these ranges and needn't reach their ends.
Inputs may be any that keep to these rules, and one draw needn't show every extreme that they name: `pivots`: entry j lies between j and 65535; the last entry is 65535.
All inputs are finite; a program needn't handle non-finite values.
Results may differ from the reference program's by a relative error of at most 0.0001.
Values sent between devices are 32-bit elements; how exact they have to be, the bound alone decides.
A program may use at most 128 MiB of HBM per device.

```python
import math
import jax
import jax.numpy as jnp
from jax import lax

M = 65536
NB = 128
PANELS = 1
COLB = 1
ROW_BLOCKS = 128
COLS = 4096
PIVOTS = 128


def pivot_list(key):
    pivot_key = jax.random.fold_in(key, 11)
    column_ids = jnp.arange(PIVOTS, dtype=jnp.int32)
    chosen = jax.random.randint(pivot_key, (PIVOTS,), column_ids, M, dtype=jnp.int32)
    return chosen.at[PIVOTS - 1].set(M - 1)


def draw_pivots(key, part):
    return pivot_list(key)


def draw_matrix(key, part):
    chosen = pivot_list(key)
    key_base = jax.random.fold_in(key, 23)
    key_diag = jax.random.fold_in(key, 29)
    key_sign = jax.random.fold_in(key, 31)
    row_ids = jnp.arange(M, dtype=jnp.int32)[:, None]
    col_ids = jnp.arange(COLS, dtype=jnp.int32)[None, :]
    leading = row_ids < PIVOTS
    base = jax.random.truncated_normal(key_base, -6.0, 6.0, (M, COLS), jnp.float32)
    base = base * jnp.where(leading, 1.0, 2.0)
    magnitude = jax.random.uniform(key_diag, (M, 1), jnp.float32, 3.0, 4.5) * math.sqrt(PIVOTS)
    sign_bits = jax.random.bernoulli(key_sign, 0.5, (M, 1))
    diagonal = jnp.where(sign_bits, magnitude, -magnitude)
    dominant = jnp.where(leading & (row_ids == col_ids), diagonal, base)

    def undo_swap(step_no, order_map):
        column_no = (PIVOTS - 1 - step_no).astype(jnp.int32)
        partner = chosen[column_no]
        value_here = order_map[column_no]
        value_there = order_map[partner]
        return order_map.at[column_no].set(value_there).at[partner].set(value_here)
    order_map = lax.fori_loop(0, PIVOTS, undo_swap, jnp.arange(M, dtype=jnp.int32))
    scrambled = jnp.take(dominant, order_map, axis=0)
    return scrambled.reshape(ROW_BLOCKS, M // (ROW_BLOCKS * NB), NB, COLB, COLS // (COLB * NB), NB)


def setup_inputs(seed: int = 0) -> dict:
    keys = jax.random.split(jax.random.key(seed), 3)
    return {
        "matrix": draw_matrix(jax.random.fold_in(keys[2], 71), 0),
        "pivots": draw_pivots(jax.random.fold_in(keys[2], 71), 0),
    }


def eliminate(square):
    size = square.shape[0]
    positions = jnp.arange(size, dtype=jnp.int32)

    def reduce_step(column_no, factors):
        column = factors[:, column_no]
        pivot_value = factors[column_no, column_no]
        below = positions > column_no
        multiplier = jnp.where(below, column / pivot_value, 0.0)
        pivot_row = jnp.where(below, factors[column_no], 0.0)
        factors = factors - multiplier[:, None] * pivot_row[None, :]
        return jnp.where(below[:, None] & (positions[None, :] == column_no), multiplier[:, None], factors)

    return lax.fori_loop(0, size, reduce_step, square)


def both_inverses(packed):
    size = packed.shape[0]
    positions = jnp.arange(size, dtype=jnp.int32)
    strict_low = jnp.where(positions[:, None] > positions[None, :], packed, 0.0)
    strict_up = jnp.where(positions[:, None] < positions[None, :], packed, 0.0)
    diag_values = jnp.sum(jnp.where(positions[:, None] == positions[None, :], packed, 0.0), axis=1)

    def row_step(step_no, inverses):
        upper_inv, lower_inv = inverses
        low_no = jnp.asarray(step_no).astype(jnp.int32)
        up_no = (size - 1 - jnp.asarray(step_no)).astype(jnp.int32)
        low_row = lax.dynamic_index_in_dim(strict_low, low_no, 0, keepdims=False)
        up_row = lax.dynamic_index_in_dim(strict_up, up_no, 0, keepdims=False)
        pivot_value = lax.dynamic_index_in_dim(diag_values, up_no, 0, keepdims=False)
        low_unit = (positions == low_no).astype(jnp.float32)
        up_unit = (positions == up_no).astype(jnp.float32)
        new_low = low_unit - jnp.dot(low_row, lower_inv, precision=lax.Precision.HIGHEST, preferred_element_type=jnp.float32)
        new_up = (up_unit - jnp.dot(up_row, upper_inv, precision=lax.Precision.HIGHEST, preferred_element_type=jnp.float32)) / pivot_value
        lower_inv = lax.dynamic_update_index_in_dim(lower_inv, new_low, low_no, 0)
        upper_inv = lax.dynamic_update_index_in_dim(upper_inv, new_up, up_no, 0)
        return (upper_inv, lower_inv)

    start = jnp.zeros((size, size), jnp.float32)
    return lax.fori_loop(0, size, row_step, (start, start))


def exchange_rows(whole, pivots, first_row, count):
    def one_swap(column_no, order_map):
        column_no = jnp.asarray(column_no).astype(jnp.int32)
        partner = pivots[column_no].astype(jnp.int32)
        value_here = order_map[column_no]
        value_there = order_map[partner]
        return order_map.at[column_no].set(value_there).at[partner].set(value_here)

    order_map = lax.fori_loop(first_row, first_row + count, one_swap, jnp.arange(whole.shape[0], dtype=jnp.int32))
    return jnp.take(whole, order_map, axis=0)


def reference(matrix, pivots):
    whole = matrix.reshape(M, COLS)
    for which in range(PANELS):
        first_row = which * NB
        after = first_row + NB
        whole = exchange_rows(whole, pivots, first_row, NB)
        packed = eliminate(whole[first_row:after, first_row:after])
        uinv, linv = both_inverses(packed)
        lower = jnp.dot(whole[after:, first_row:after], uinv, precision=lax.Precision.HIGHEST, preferred_element_type=jnp.float32)
        urows = jnp.dot(linv, whole[first_row:after, after:], precision=lax.Precision.HIGHEST, preferred_element_type=jnp.float32)
        trailing = whole[after:, after:] - jnp.dot(lower, urows, precision=lax.Precision.HIGHEST, preferred_element_type=jnp.float32)
        whole = whole.at[after:, after:].set(trailing)
        whole = whole.at[first_row:after, first_row:after].set(packed)
        whole = whole.at[after:, first_row:after].set(lower)
        whole = whole.at[first_row:after, after:].set(urows)
    return whole.reshape(matrix.shape)
```

```python
import functools

import jax
import jax.numpy as jnp
from jax import lax
from jax.experimental import pallas as pl
from jax.experimental.pallas import tpu as pltpu
from jax.sharding import PartitionSpec as P

MESH = pl.DeviceIdType.MESH
F32 = jnp.float32
BF16 = jnp.bfloat16
NB = 128
SIDE = 4
TREES = 4
STEPS = ((1, 0), (-1, 0), (0, 1), (0, -1))
SENDERS = ((0, 4, 8, 11, 5, 6, 9, 10), (7, 5, 6), (4, 5), (4, 8))
DEPTHS = (0, 3, 4, 3, 1, 2, 3, 2, 2, 3, 4, 3, 3, 4, 5, 4)
MAX_DEPTH = max(DEPTHS)
SKEW = 6
CHUNK = 128
PIECES = 4
READY = 38
VMEM_MIB = 40


def one_of(value, places):
    found = value == places[0]
    for place in places[1:]:
        found = jnp.logical_or(found, value == place)
    return found


def turn(step, times):
    for _ in range(times):
        step = (-step[1], step[0])
    return step


def eliminate_and_invert(a_ref, inv_ref):
    n, b = NB, 8
    lanes1 = lax.broadcasted_iota(jnp.int32, (1, n), 1)
    lanes8 = lax.broadcasted_iota(jnp.int32, (b, n), 1)
    subl = lax.broadcasted_iota(jnp.int32, (b, n), 0)
    rows = lax.broadcasted_iota(jnp.int32, (n, n), 0)
    lanes = lax.broadcasted_iota(jnp.int32, (n, n), 1)
    inv_ref[...] = jnp.zeros((n, n), F32)

    def block(k, carry):
        c0 = pl.multiple_of(k * b, b)

        def pick(x, j):
            return jnp.take_along_axis(x, jnp.full(x.shape, c0 + j, jnp.int32), axis=1)

        row = a_ref[pl.ds(c0, b), :]
        irow = inv_ref[pl.ds(c0, b), :]
        cols = [pick(row, j) for j in range(b)]
        recs, us, prow, pinv, gs = [], {}, [], [], []
        for s in range(b):
            r = 1.0 / jnp.broadcast_to(cols[s][s : s + 1], (b, n))
            recs.append(r[0:1])
            g = jnp.where(subl > s, cols[s] * r, 0.0)
            gs.append(g)
            for j in range(s + 1, b):
                us[s, j] = cols[j][s : s + 1]
                cols[j] = cols[j] - g * us[s, j]
            ar = jnp.where(lanes1 > c0 + s, row[s : s + 1], 0.0)
            row = row - g * ar
            ir = jnp.where(lanes1 == c0 + s, 1.0, irow[s : s + 1])
            irow = irow - g * ir
            prow.append(ar)
            pinv.append(ir)
        for s in range(b):
            row = jnp.where((lanes8 == c0 + s) & (subl > s), gs[s], row)
        whole = a_ref[...]
        inverse = inv_ref[...]
        below = rows >= c0 + b
        own = jnp.where(rows == lanes, 1.0, 0.0)
        mix = jnp.where(below, whole, jnp.where(rows < c0, inverse, own))
        mult = []
        for j in range(b):
            c = pick(mix, j)
            for s in range(j):
                c = c - mult[s] * us[s, j]
            mult.append(c * recs[j])
        upd = whole
        iupd = jnp.where((rows >= c0) & (rows < c0 + b), 0.0, inverse)
        for s in range(b):
            upd = upd - mult[s] * prow[s]
            iupd = iupd - mult[s] * jnp.where(below, pinv[s], prow[s])
        for s in range(b):
            at = lanes == c0 + s
            upd = jnp.where(at, mult[s], upd)
            iupd = jnp.where(at & jnp.logical_not(below), mult[s], iupd)
        a_ref[...] = jnp.where(below, upd, whole)
        inv_ref[...] = iupd
        a_ref[pl.ds(c0, b), :] = row
        inv_ref[pl.ds(c0, b), :] = jnp.where(lanes8 < c0 + subl, irow, inv_ref[pl.ds(c0, b), :])
        return carry

    lax.fori_loop(0, n // b, block, 0)


def exchange_kernel(
    piv_s, piv_v, mat, held, fix,
    panel, contrib, xbuf, dbuf, moved, diag, low_rows, inv, packed, right_upper, right_rows, src_v, src_s,
    load_sem, piece_sem, src_sem, recv_sem, tree_sem, part_sem, x_send, x_recv, d_send, d_recv,
    z_send, y_send, f_recv, c_send, c_recv,
):
    rows_local = held.shape[0]
    share = rows_local // TREES
    chunks = share // CHUNK
    per_piece = chunks // PIECES
    piece_rows = per_piece * CHUNK
    px = lax.axis_index("prow")
    pc = lax.axis_index("pcol")
    core = lax.rem(pc, 2)
    chip = lax.div(pc, 2)
    y = lax.div(chip, SIDE)
    z = lax.rem(chip, SIDE)
    is_root = pc == 0
    is_root1 = pc == 1
    partner = (px, pc + 1 - 2 * core)

    def pcol_of(yy, zz):
        return (lax.rem(yy + SIDE, SIDE) * SIDE + lax.rem(zz + SIDE, SIDE)) * 2 + core

    x_peers = [(lax.rem(px + k, SIDE), pc) for k in range(1, SIDE)]
    y_peers = [(px, pcol_of(y + k, z)) for k in range(1, SIDE)]
    z_peers = [(px, pcol_of(y, z + k)) for k in range(1, SIDE)]
    cross = [(lax.rem(px + k, SIDE), 1 - pc) for k in range(1, SIDE)]

    def remote(src, dst, send, recv, where):
        return pltpu.make_async_remote_copy(
            src_ref=src, dst_ref=dst, send_sem=send, recv_sem=recv, device_id=where, device_id_type=MESH
        )

    hold = pltpu.make_async_copy(mat, held, load_sem)
    pieces = []
    for q in range(PIECES):
        for t in range(TREES):
            part = pl.ds(t * share + q * piece_rows, piece_rows)
            pieces.append(pltpu.make_async_copy(mat.at[part], panel.at[part], piece_sem.at[q * TREES + t]))

    @pl.when(is_root)
    def _():
        for piece in pieces:
            piece.start()

    @pl.when(jnp.logical_not(is_root))
    def _():
        hold.start()

    barrier = pltpu.get_barrier_semaphore()
    for where in x_peers + y_peers + z_peers + [partner]:
        pl.semaphore_signal(barrier, inc=1, device_id=where, device_id_type=MESH)

    @pl.when(pc < 2)
    def _():
        for where in cross:
            pl.semaphore_signal(barrier, inc=1, device_id=where, device_id_type=MESH)

    which = lax.broadcasted_iota(jnp.int32, (8, NB), 0)
    sources = jnp.where(which == 0, lax.broadcasted_iota(jnp.int32, (8, NB), 1), piv_v[...])

    def back(step, sources):
        column = NB - 1 - step
        other = piv_s[column]
        return jnp.where(sources == column, other, jnp.where(sources == other, column, sources))

    src_v[...] = lax.fori_loop(0, NB, back, sources)
    to_scalars = pltpu.make_async_copy(src_v, src_s, src_sem)
    to_scalars.start()

    @pl.when(pc < 2)
    def _():
        pl.semaphore_wait(barrier, 13)

    @pl.when(pc >= 2)
    def _():
        pl.semaphore_wait(barrier, 10)

    feeds, depth, targets = [], [], []
    for t in range(TREES):
        yy, zz = y, z
        for _ in range(t):
            yy, zz = zz, lax.rem(SIDE - yy, SIDE)
        place = yy * SIDE + zz
        feeds.append([one_of(place, SENDERS[d]) for d in range(4)])
        level = 0
        for where in range(1, SIDE * SIDE):
            level = level + jnp.where(place == where, DEPTHS[where], 0)
        depth.append(level)
        targets.append([])
        for d in range(4):
            dy, dz = turn(STEPS[d], t)
            targets[t].append((px, pcol_of(y + dy, z + dz)))

    def chunk_at(t, c):
        return panel.at[pl.ds(pl.multiple_of(t * share + c * CHUNK, CHUNK), CHUNK)]

    def forward(t, c):
        block = chunk_at(t, c)
        arrival = recv_sem.at[t * chunks + c]
        for d in range(4):

            @pl.when(feeds[t][d])
            def _():
                remote(block, block, tree_sem.at[t * 4 + d], arrival, targets[t][d]).start()

        remote(block, block, part_sem.at[t], arrival, partner).start()

    def forward_range(lo, hi):
        def one(c, carry):
            for t in range(TREES):
                forward(t, c)
            return carry

        lax.fori_loop(lo, hi, one, 0)

    to_scalars.wait()

    def gather_from(rows_ref):
        def gather(g, carry):
            for r in range(2):
                base = pl.multiple_of(g * 8, 8)
                found = []
                for s in range(8):
                    source = src_s[r, g * 8 + s]
                    block = lax.div(source, NB)
                    mine = lax.rem(block, SIDE) == px
                    local = lax.div(block, SIDE) * NB + lax.rem(source, NB)
                    row = rows_ref[pl.ds(jnp.where(mine, local, 0), 1), :]
                    found.append(jnp.where(mine, row, 0.0))
                contrib[pl.ds(r * NB + base, 8), :] = jnp.concatenate(found, axis=0)
            return carry

        lax.fori_loop(0, NB // 8, gather, 0)

    @pl.when(is_root)
    def _():
        for piece in pieces[:TREES]:
            piece.wait()
        forward_range(0, per_piece)
        for piece in pieces[TREES:]:
            piece.wait()
        gather_from(panel)

    @pl.when(jnp.logical_not(is_root))
    def _():
        hold.wait()
        gather_from(held)

    d_copies = []
    for k in range(SIDE):
        where = (lax.rem(px + k, SIDE), pc + 1)
        d_copies.append(remote(contrib, dbuf.at[px], d_send.at[k], d_recv.at[px], where))

    @pl.when(is_root)
    def _():
        for copy in d_copies:
            copy.start()

    x_copies = [
        remote(contrib, xbuf.at[px], x_send.at[k], x_recv.at[px], x_peers[k]) for k in range(SIDE - 1)
    ]
    for copy in x_copies:
        copy.start()

    def arrived(ref, sem):
        pltpu.make_async_copy(ref, ref, sem).wait()

    def receive_moved():
        total = contrib[...]
        for k in range(1, SIDE):
            slot = lax.rem(px + k, SIDE)
            arrived(xbuf.at[slot], x_recv.at[slot])
            total = total + xbuf[slot]
        moved[...] = total

    def take_factors():
        receive_moved()
        upper, urows = factors(inv[...], moved[pl.ds(0, NB), :])
        right_upper[...] = right_side(upper)
        right_rows[...] = right_side(urows)

    def update(starts, size):
        places = [pl.ds(pl.multiple_of(start, CHUNK), size) for start in starts]
        old = [held[place, :] for place in places]
        upper, rows = right_upper[...], right_rows[...]
        lows = [product(panel[place, :], upper) for place in places]
        for place, x, low in zip(places, old, lows):
            held[place, :] = jnp.where(is_root, low, x - product(low, rows))

    def update_group(g, width):
        update([t * share + g * CHUNK for t in range(TREES)], width * CHUNK)

    def update_pairs(lo, hi):
        def one(m, carry):
            update_group(m * 2, 2)
            return carry

        lax.fori_loop(lo // 2, hi // 2, one, 0)

    @pl.when(is_root)
    def _():
        forward_range(per_piece, chunks)
        arrived(packed, c_recv.at[1])
        arrived(inv, c_recv.at[2])
        take_factors()
        update_pairs(0, chunks)

    steps = chunks + SKEW * MAX_DEPTH
    ready = min(READY, steps)
    done = min(steps - ready, chunks)
    done -= done % 2

    @pl.when(jnp.logical_and(core == 0, jnp.logical_not(is_root)))
    def _():
        def relay(i, carry):
            for t in range(TREES):
                c = i - SKEW * depth[t]

                @pl.when(jnp.logical_and(c >= 0, c < chunks))
                def _():
                    arrived(chunk_at(t, c), recv_sem.at[t * chunks + c])
                    forward(t, c)

            return carry

        def relay_and_update(i, carry):
            relay(i, carry)
            update_group(i - ready, 1)
            return carry

        lax.fori_loop(0, ready, relay, 0)
        arrived(packed, c_recv.at[1])
        arrived(inv, c_recv.at[2])
        take_factors()
        lax.fori_loop(ready, ready + done, relay_and_update, 0)
        lax.fori_loop(ready + done, steps, relay, 0)
        update_pairs(done, chunks)

    z_copies = [remote(diag, diag, z_send.at[k], f_recv.at[0], z_peers[k]) for k in range(3)]
    z_copies += [remote(low_rows, low_rows, z_send.at[3 + k], f_recv.at[1], z_peers[k]) for k in range(3)]
    y_copies = [remote(diag, diag, y_send.at[k], f_recv.at[0], y_peers[k]) for k in range(3)]
    y_copies += [remote(low_rows, low_rows, y_send.at[3 + k], f_recv.at[1], y_peers[k]) for k in range(3)]
    c_copies = [
        remote(low_rows, low_rows, c_send.at[0], c_recv.at[0], partner),
        remote(packed, packed, c_send.at[1], c_recv.at[1], partner),
        remote(inv, inv, c_send.at[2], c_recv.at[2], partner),
    ]

    @pl.when(core == 1)
    def _():
        @pl.when(is_root1)
        def _():
            for k in range(SIDE):
                arrived(dbuf.at[k], d_recv.at[k])
            total = dbuf[0] + dbuf[1] + dbuf[2] + dbuf[3]
            diag[...] = total[:NB]
            low_rows[...] = total[NB:]
            for k in range(3):
                z_copies[k].start()
            for k in range(3):
                y_copies[k].start()
            for k in range(3):
                z_copies[3 + k].start()
            for k in range(3):
                y_copies[3 + k].start()

        @pl.when(jnp.logical_not(is_root1))
        def _():
            arrived(diag, f_recv.at[0])

            @pl.when(y == 0)
            def _():
                for k in range(3):
                    y_copies[k].start()
                arrived(low_rows, f_recv.at[1])
                for k in range(3):
                    y_copies[3 + k].start()

        packed[...] = diag[...]
        eliminate_and_invert(packed, inv)
        c_copies[1].start()
        c_copies[2].start()

        @pl.when(y != 0)
        def _():
            arrived(low_rows, f_recv.at[1])

        c_copies[0].start()
        take_factors()

        def receive(m, carry):
            for i in (2 * m, 2 * m + 1):
                for t in range(TREES):
                    arrived(chunk_at(t, i), recv_sem.at[t * chunks + i])
            update_group(2 * m, 2)
            return carry

        lax.fori_loop(0, chunks // 2, receive, 0)

        for copy in c_copies:
            copy.wait_send()

        @pl.when(is_root1)
        def _():
            for copy in z_copies:
                copy.wait_send()

        @pl.when(y == 0)
        def _():
            for copy in y_copies:
                copy.wait_send()

    @pl.when(core == 0)
    def _():
        arrived(low_rows, c_recv.at[0])
        for t in range(TREES):
            sent = panel.at[pl.ds(t * share, share)]
            for d in range(4):

                @pl.when(feeds[t][d])
                def _():
                    remote(sent, sent, tree_sem.at[t * 4 + d], recv_sem.at[0], partner).wait_send()

            remote(sent, sent, part_sem.at[t], recv_sem.at[0], partner).wait_send()

        @pl.when(is_root)
        def _():
            for copy in d_copies:
                copy.wait_send()

    low = product(low_rows[...], right_upper[...])
    fix[...] = jnp.where(is_root, low, moved[pl.ds(NB, NB), :] - product(low, right_rows[...]))

    @pl.when(px == 0)
    def _():
        lower = moved[pl.ds(0, NB), :]
        urows = factors(inv[...], lower)[1]
        held[pl.ds(0, NB), :] = jnp.where(is_root, packed[...], urows)

    for copy in x_copies:
        copy.wait_send()


def split(x):
    high = x.astype(BF16)
    return high, (x - high.astype(F32)).astype(BF16)


def right_side(x):
    high, low = split(x)
    return jnp.concatenate(
        [jnp.concatenate([high, low], axis=1), jnp.concatenate([high, jnp.zeros_like(low)], axis=1)], axis=0
    )


def product(x, right):
    high, low = split(x)
    both = jnp.dot(jnp.concatenate([high, low], axis=1), right, preferred_element_type=F32)
    return both[:, :NB] + both[:, NB:]


def factors(inv, moved_top):
    rows = lax.broadcasted_iota(jnp.int32, (NB, NB), 0)
    lanes = lax.broadcasted_iota(jnp.int32, (NB, NB), 1)
    upper = jnp.where(rows <= lanes, inv, 0.0)
    lower = jnp.where(rows > lanes, inv, jnp.where(rows == lanes, 1.0, 0.0))
    urows = jnp.dot(lower, moved_top, precision=lax.Precision.HIGHEST, preferred_element_type=F32)
    return upper, urows


def finish_kernel(piv_s, held, fix, out, store_sem, row_sem):
    blocks = store_sem.shape[0]
    size = held.shape[0] // blocks
    px = lax.axis_index("prow")
    stores = []
    for b in range(blocks):
        part = pl.ds(b * size, size)
        stores.append(pltpu.make_async_copy(held.at[part], out.at[part], store_sem.at[b]))
    for store in stores:
        store.start()
    for store in stores:
        store.wait()

    def row_copy(j):
        target = piv_s[j]
        place = lax.div(target, NB)
        mine = jnp.logical_and(lax.rem(place, SIDE) == px, place > 0)
        local = lax.div(place, SIDE) * NB + lax.rem(target, NB)
        return mine, pltpu.make_async_copy(fix.at[pl.ds(j, 1)], out.at[pl.ds(local, 1)], row_sem)

    def start(j, carry):
        mine, copy = row_copy(j)

        @pl.when(mine)
        def _():
            copy.start()

        return carry

    def finish(j, carry):
        mine, copy = row_copy(j)

        @pl.when(mine)
        def _():
            copy.wait()

        return carry

    lax.fori_loop(0, NB, start, 0)
    lax.fori_loop(0, NB, finish, 0)


def local(matrix, pivots):
    rows_local = matrix.shape[0] * matrix.shape[2]
    held = matrix.reshape(rows_local, NB)
    chunks = rows_local // CHUNK
    smem = pl.BlockSpec(memory_space=pltpu.SMEM)
    vmem = pl.BlockSpec(memory_space=pltpu.VMEM)
    hbm = pl.BlockSpec(memory_space=pl.ANY)
    square = pltpu.VMEM((NB, NB), F32)
    dma = pltpu.SemaphoreType.DMA
    changed, fix = pl.pallas_call(
        exchange_kernel,
        out_shape=(
            jax.ShapeDtypeStruct((rows_local, NB), F32),
            jax.ShapeDtypeStruct((NB, NB), F32),
        ),
        in_specs=[smem, vmem, hbm],
        out_specs=(vmem,) * 2,
        scratch_shapes=[
            pltpu.VMEM((rows_local, NB), F32),
            pltpu.VMEM((2 * NB, NB), F32),
            pltpu.VMEM((SIDE, 2 * NB, NB), F32),
            pltpu.VMEM((SIDE, 2 * NB, NB), F32),
            pltpu.VMEM((2 * NB, NB), F32),
            square,
            square,
            square,
            square,
            pltpu.VMEM((2 * NB, 2 * NB), BF16),
            pltpu.VMEM((2 * NB, 2 * NB), BF16),
            pltpu.VMEM((8, NB), jnp.int32),
            pltpu.SMEM((8, NB), jnp.int32),
            dma,
            dma((PIECES * TREES,)),
            dma,
            dma((chunks,)),
            dma((TREES * 4,)),
            dma((TREES,)),
            dma((SIDE - 1,)),
            dma((SIDE,)),
            dma((SIDE,)),
            dma((SIDE,)),
            dma((6,)),
            dma((6,)),
            dma((2,)),
            dma((3,)),
            dma((3,)),
        ],
        compiler_params=pltpu.CompilerParams(
            collective_id=0, has_side_effects=True, vmem_limit_bytes=VMEM_MIB * 2**20
        ),
    )(pivots, pivots.reshape(1, NB), held)
    out = pl.pallas_call(
        finish_kernel,
        out_shape=jax.ShapeDtypeStruct((rows_local, NB), F32),
        in_specs=[smem, vmem, vmem],
        out_specs=hbm,
        scratch_shapes=[dma((4,)), dma],
        compiler_params=pltpu.CompilerParams(vmem_limit_bytes=4 * 2**20),
    )(pivots, changed, fix)
    return out.reshape(matrix.shape)


def solution(mesh):
    return jax.shard_map(
        local,
        mesh=mesh,
        in_specs=(P(None, "prow", None, None, "pcol", None), P()),
        out_specs=P(None, "prow", None, None, "pcol", None),
        check_vma=False,
    )
```

```python
import functools

import jax
import jax.numpy as jnp
from jax import lax
from jax.experimental import pallas as pl
from jax.experimental.pallas import tpu as pltpu
from jax.sharding import PartitionSpec as P

MESH = pl.DeviceIdType.MESH
F32 = jnp.float32
BF16 = jnp.bfloat16
NB = 128
SIDE = 4
TREES = 4
STEPS = ((1, 0), (-1, 0), (0, 1), (0, -1))
SENDERS = (
    ((0, 4, 8, 9, 10, 11), (5, 6, 7), (4, 5, 8, 9), (4, 8)),
    ((13, 14, 15), (0, 8, 9, 10, 11, 12, 13, 14, 15), (12, 13), (12,)),
    ((1, 2, 5, 6), (1, 2), (0, 1, 2, 6, 10, 14), (5, 9, 13)),
    ((3, 7), (3,), (7, 11, 15), (0, 2, 3, 6, 7, 10, 11, 14, 15)),
)
PLAIN, ROUND = 5, 6
CHUNK = 128
PIECES = 4
EARLY = 24
READY = 36
WIDE = 4
VMEM_MIB = 40


def one_of(value, places):
    found = value < 0
    for place in places:
        found = jnp.logical_or(found, value == place)
    return found


def lags(tree):
    lag = {0: 0}
    while len(lag) < SIDE * SIDE:
        for d, places in enumerate(SENDERS[tree]):
            for place in places:
                if place in lag:
                    y, z = place // SIDE + STEPS[d][0], place % SIDE + STEPS[d][1]
                    plain = 0 <= y < SIDE and 0 <= z < SIDE
                    lag[y % SIDE * SIDE + z % SIDE] = lag[place] + (PLAIN if plain else ROUND)
    return [lag[place] for place in range(SIDE * SIDE)]


def eliminate_and_invert(a_ref, inv_ref):
    n, b = NB, 8
    lanes1 = lax.broadcasted_iota(jnp.int32, (1, n), 1)
    lanes8 = lax.broadcasted_iota(jnp.int32, (b, n), 1)
    subl = lax.broadcasted_iota(jnp.int32, (b, n), 0)
    rows = lax.broadcasted_iota(jnp.int32, (n, n), 0)
    lanes = lax.broadcasted_iota(jnp.int32, (n, n), 1)
    inv_ref[...] = jnp.zeros((n, n), F32)

    def block(k, carry):
        c0 = pl.multiple_of(k * b, b)

        def pick(x, j):
            return jnp.take_along_axis(x, jnp.full(x.shape, c0 + j, jnp.int32), axis=1)

        row = a_ref[pl.ds(c0, b), :]
        irow = inv_ref[pl.ds(c0, b), :]
        cols = [pick(row, j) for j in range(b)]
        recs, us, prow, pinv, gs = [], {}, [], [], []
        for s in range(b):
            r = 1.0 / jnp.broadcast_to(cols[s][s : s + 1], (b, n))
            recs.append(r[0:1])
            g = jnp.where(subl > s, cols[s] * r, 0.0)
            gs.append(g)
            for j in range(s + 1, b):
                us[s, j] = cols[j][s : s + 1]
                cols[j] = cols[j] - g * us[s, j]
            ar = jnp.where(lanes1 > c0 + s, row[s : s + 1], 0.0)
            row = row - g * ar
            ir = jnp.where(lanes1 == c0 + s, 1.0, irow[s : s + 1])
            irow = irow - g * ir
            prow.append(ar)
            pinv.append(ir)
        for s in range(b):
            row = jnp.where((lanes8 == c0 + s) & (subl > s), gs[s], row)
        whole = a_ref[...]
        inverse = inv_ref[...]
        below = rows >= c0 + b
        own = jnp.where(rows == lanes, 1.0, 0.0)
        mix = jnp.where(below, whole, jnp.where(rows < c0, inverse, own))
        mult = []
        for j in range(b):
            c = pick(mix, j)
            for s in range(j):
                c = c - mult[s] * us[s, j]
            mult.append(c * recs[j])
        upd = whole
        iupd = jnp.where((rows >= c0) & (rows < c0 + b), 0.0, inverse)
        for s in range(b):
            upd = upd - mult[s] * prow[s]
            iupd = iupd - mult[s] * jnp.where(below, pinv[s], prow[s])
        for s in range(b):
            at = lanes == c0 + s
            upd = jnp.where(at, mult[s], upd)
            iupd = jnp.where(at & jnp.logical_not(below), mult[s], iupd)
        a_ref[...] = jnp.where(below, upd, whole)
        inv_ref[...] = iupd
        a_ref[pl.ds(c0, b), :] = row
        inv_ref[pl.ds(c0, b), :] = jnp.where(lanes8 < c0 + subl, irow, inv_ref[pl.ds(c0, b), :])
        return carry

    lax.fori_loop(0, n // b, block, 0)


def exchange_kernel(
    pivots, mat, held, fix,
    panel, contrib, xbuf, dbuf, moved, diag, low_rows, inv, packed, right_upper, right_rows, src_v, src_s, piv_v, piv_s,
    pivot_sem, load_sem, piece_sem, src_sem, recv_sem, tree_sem, part_sem, x_send, x_recv, d_send, d_recv,
    z_send, y_send, f_recv, c_send, c_recv,
):
    rows_local = held.shape[0]
    share = rows_local // TREES
    chunks = share // CHUNK
    per_piece = chunks // PIECES
    piece_rows = per_piece * CHUNK
    px = lax.axis_index("prow")
    pc = lax.axis_index("pcol")
    core = lax.rem(pc, 2)
    chip = lax.div(pc, 2)
    y = lax.div(chip, SIDE)
    z = lax.rem(chip, SIDE)
    is_root = pc == 0
    is_root1 = pc == 1
    partner = (px, pc + 1 - 2 * core)

    def pcol_of(yy, zz):
        return (lax.rem(yy + SIDE, SIDE) * SIDE + lax.rem(zz + SIDE, SIDE)) * 2 + core

    x_peers = [(lax.rem(px + k, SIDE), pc) for k in range(1, SIDE)]
    y_peers = [(px, pcol_of(y + k, z)) for k in range(1, SIDE)]
    z_peers = [(px, pcol_of(y, z + k)) for k in range(1, SIDE)]
    cross = [(lax.rem(px + k, SIDE), 1 - pc) for k in range(1, SIDE)]

    def remote(src, dst, send, recv, where):
        return pltpu.make_async_remote_copy(
            src_ref=src, dst_ref=dst, send_sem=send, recv_sem=recv, device_id=where, device_id_type=MESH
        )

    pivot_copies = [
        pltpu.make_async_copy(pivots, piv_s, pivot_sem.at[0]),
        pltpu.make_async_copy(pivots, piv_v, pivot_sem.at[1]),
    ]
    for copy in pivot_copies:
        copy.start()

    hold = pltpu.make_async_copy(mat, held, load_sem)
    pieces = []
    for q in range(PIECES):
        for t in range(TREES):
            part = pl.ds(t * share + q * piece_rows, piece_rows)
            pieces.append(pltpu.make_async_copy(mat.at[part], panel.at[part], piece_sem.at[q * TREES + t]))

    @pl.when(is_root)
    def _():
        for piece in pieces:
            piece.start()

    @pl.when(jnp.logical_not(is_root))
    def _():
        hold.start()

    barrier = pltpu.get_barrier_semaphore()
    for where in x_peers + y_peers + z_peers + [partner]:
        pl.semaphore_signal(barrier, inc=1, device_id=where, device_id_type=MESH)

    @pl.when(pc < 2)
    def _():
        for where in cross:
            pl.semaphore_signal(barrier, inc=1, device_id=where, device_id_type=MESH)

    for copy in pivot_copies:
        copy.wait()
    which = lax.broadcasted_iota(jnp.int32, (8, NB), 0)
    sources = jnp.where(which == 0, lax.broadcasted_iota(jnp.int32, (8, NB), 1), piv_v[...])

    def back(step, sources):
        column = NB - 1 - step
        other = piv_s[0, column]
        return jnp.where(sources == column, other, jnp.where(sources == other, column, sources))

    src_v[...] = lax.fori_loop(0, NB, back, sources)
    to_scalars = pltpu.make_async_copy(src_v, src_s, src_sem)
    to_scalars.start()

    @pl.when(pc < 2)
    def _():
        pl.semaphore_wait(barrier, 13)

    @pl.when(pc >= 2)
    def _():
        pl.semaphore_wait(barrier, 10)

    feeds, delay = [], []
    targets = [(px, pcol_of(y + dy, z + dz)) for dy, dz in STEPS]
    for t in range(TREES):
        feeds.append([one_of(chip, SENDERS[t][d]) for d in range(4)])
        late = 0
        for place, lag in enumerate(lags(t)):
            late = late + jnp.where(chip == place, lag, 0)
        delay.append(late)

    def chunk_at(t, c):
        return panel.at[pl.ds(pl.multiple_of(t * share + c * CHUNK, CHUNK), CHUNK)]

    def forward(t, c):
        block = chunk_at(t, c)
        arrival = recv_sem.at[t * chunks + c]
        for d in range(4):

            @pl.when(feeds[t][d])
            def _():
                remote(block, block, tree_sem.at[t * 4 + d], arrival, targets[d]).start()

        remote(block, block, part_sem.at[t], arrival, partner).start()

    def forward_range(lo, hi):
        def one(c, carry):
            for t in range(TREES):
                forward(t, c)
            return carry

        lax.fori_loop(lo, hi, one, 0)

    to_scalars.wait()

    def gather_from(rows_ref):
        def gather(g, carry):
            for r in range(2):
                base = pl.multiple_of(g * 8, 8)
                found = []
                for s in range(8):
                    source = src_s[r, g * 8 + s]
                    block = lax.div(source, NB)
                    mine = lax.rem(block, SIDE) == px
                    local = lax.div(block, SIDE) * NB + lax.rem(source, NB)
                    row = rows_ref[pl.ds(jnp.where(mine, local, 0), 1), :]
                    found.append(jnp.where(mine, row, 0.0))
                contrib[pl.ds(r * NB + base, 8), :] = jnp.concatenate(found, axis=0)
            return carry

        lax.fori_loop(0, NB // 8, gather, 0)

    @pl.when(is_root)
    def _():
        for piece in pieces[:TREES]:
            piece.wait()
        forward_range(0, per_piece)
        for piece in pieces[TREES:]:
            piece.wait()
        gather_from(panel)

    @pl.when(jnp.logical_not(is_root))
    def _():
        hold.wait()
        gather_from(held)

    d_copies = []
    for k in range(SIDE):
        where = (lax.rem(px + k, SIDE), pc + 1)
        d_copies.append(remote(contrib, dbuf.at[px], d_send.at[k], d_recv.at[px], where))

    @pl.when(is_root)
    def _():
        for copy in d_copies:
            copy.start()

    x_copies = [
        remote(contrib, xbuf.at[px], x_send.at[k], x_recv.at[px], x_peers[k]) for k in range(SIDE - 1)
    ]
    for copy in x_copies:
        copy.start()

    def arrived(ref, sem):
        pltpu.make_async_copy(ref, ref, sem).wait()

    def receive_moved():
        total = contrib[...]
        for k in range(1, SIDE):
            slot = lax.rem(px + k, SIDE)
            arrived(xbuf.at[slot], x_recv.at[slot])
            total = total + xbuf[slot]
        moved[...] = total

    def take_factors():
        upper, urows = factors(inv[...], moved[pl.ds(0, NB), :])
        right_upper[...] = right_side(upper)
        right_rows[...] = right_side(urows)

    def update(starts, size):
        places = [pl.ds(pl.multiple_of(start, CHUNK), size) for start in starts]
        old = [held[place, :] for place in places]
        upper, rows = right_upper[...], right_rows[...]
        lows = [product(panel[place, :], upper) for place in places]
        for place, x, low in zip(places, old, lows):
            held[place, :] = jnp.where(is_root, low, x - product(low, rows))

    def update_group(g, width):
        update([t * share + g * CHUNK for t in range(TREES)], width * CHUNK)

    def update_rest(lo, hi):
        def one(m, carry):
            update_group(m * WIDE, WIDE)
            return carry

        lax.fori_loop(lo // WIDE, hi // WIDE, one, 0)

    @pl.when(is_root)
    def _():
        forward_range(per_piece, chunks)
        receive_moved()
        arrived(packed, c_recv.at[1])
        arrived(inv, c_recv.at[2])
        take_factors()
        update_rest(0, chunks)

    steps = chunks + max(max(lags(t)) for t in range(TREES))
    ready = min(READY, steps)
    done = min(steps - ready, chunks)
    ready += done % WIDE
    done -= done % WIDE

    @pl.when(jnp.logical_and(core == 0, jnp.logical_not(is_root)))
    def _():
        def relay(i, carry):
            for t in range(TREES):
                c = i - delay[t]

                @pl.when(jnp.logical_and(c >= 0, c < chunks))
                def _():
                    arrived(chunk_at(t, c), recv_sem.at[t * chunks + c])
                    forward(t, c)

            return carry

        def relay_and_update(i, carry):
            relay(i, carry)
            update_group(i - ready, 1)
            return carry

        early = min(EARLY, ready)
        lax.fori_loop(0, early, relay, 0)
        receive_moved()
        lax.fori_loop(early, ready, relay, 0)
        arrived(packed, c_recv.at[1])
        arrived(inv, c_recv.at[2])
        take_factors()
        lax.fori_loop(ready, ready + done, relay_and_update, 0)
        lax.fori_loop(ready + done, steps, relay, 0)
        update_rest(done, chunks)

    z_copies = [remote(diag, diag, z_send.at[k], f_recv.at[0], z_peers[k]) for k in range(3)]
    z_copies += [remote(low_rows, low_rows, z_send.at[3 + k], f_recv.at[1], z_peers[k]) for k in range(3)]
    y_copies = [remote(diag, diag, y_send.at[k], f_recv.at[0], y_peers[k]) for k in range(3)]
    y_copies += [remote(low_rows, low_rows, y_send.at[3 + k], f_recv.at[1], y_peers[k]) for k in range(3)]
    c_copies = [
        remote(low_rows, low_rows, c_send.at[0], c_recv.at[0], partner),
        remote(packed, packed, c_send.at[1], c_recv.at[1], partner),
        remote(inv, inv, c_send.at[2], c_recv.at[2], partner),
    ]

    @pl.when(core == 1)
    def _():
        @pl.when(is_root1)
        def _():
            for k in range(SIDE):
                arrived(dbuf.at[k], d_recv.at[k])
            total = dbuf[0] + dbuf[1] + dbuf[2] + dbuf[3]
            diag[...] = total[:NB]
            low_rows[...] = total[NB:]
            for k in range(3):
                z_copies[k].start()
            for k in range(3):
                y_copies[k].start()
            for k in range(3):
                z_copies[3 + k].start()
            for k in range(3):
                y_copies[3 + k].start()

        @pl.when(jnp.logical_not(is_root1))
        def _():
            arrived(diag, f_recv.at[0])

            @pl.when(y == 0)
            def _():
                for k in range(3):
                    y_copies[k].start()
                arrived(low_rows, f_recv.at[1])
                for k in range(3):
                    y_copies[3 + k].start()

        packed[...] = diag[...]
        eliminate_and_invert(packed, inv)
        c_copies[1].start()
        c_copies[2].start()

        @pl.when(y != 0)
        def _():
            arrived(low_rows, f_recv.at[1])

        c_copies[0].start()
        receive_moved()
        take_factors()

        def receive(m, carry):
            for i in (2 * m, 2 * m + 1):
                for t in range(TREES):
                    arrived(chunk_at(t, i), recv_sem.at[t * chunks + i])
            update_group(2 * m, 2)
            return carry

        lax.fori_loop(0, chunks // 2, receive, 0)

        for copy in c_copies:
            copy.wait_send()

        @pl.when(is_root1)
        def _():
            for copy in z_copies:
                copy.wait_send()

        @pl.when(y == 0)
        def _():
            for copy in y_copies:
                copy.wait_send()

    @pl.when(core == 0)
    def _():
        arrived(low_rows, c_recv.at[0])
        for t in range(TREES):
            sent = panel.at[pl.ds(t * share, share)]
            for d in range(4):

                @pl.when(feeds[t][d])
                def _():
                    remote(sent, sent, tree_sem.at[t * 4 + d], recv_sem.at[0], partner).wait_send()

            remote(sent, sent, part_sem.at[t], recv_sem.at[0], partner).wait_send()

        @pl.when(is_root)
        def _():
            for copy in d_copies:
                copy.wait_send()

    low = product(low_rows[...], right_upper[...])
    fix[...] = jnp.where(is_root, low, moved[pl.ds(NB, NB), :] - product(low, right_rows[...]))

    @pl.when(px == 0)
    def _():
        lower = moved[pl.ds(0, NB), :]
        urows = factors(inv[...], lower)[1]
        held[pl.ds(0, NB), :] = jnp.where(is_root, packed[...], urows)

    for copy in x_copies:
        copy.wait_send()


def split(x):
    high = x.astype(BF16)
    return high, (x - high.astype(F32)).astype(BF16)


def right_side(x):
    high, low = split(x)
    return jnp.concatenate(
        [jnp.concatenate([high, low], axis=1), jnp.concatenate([high, jnp.zeros_like(low)], axis=1)], axis=0
    )


def product(x, right):
    high, low = split(x)
    both = jnp.dot(jnp.concatenate([high, low], axis=1), right, preferred_element_type=F32)
    return both[:, :NB] + both[:, NB:]


def factors(inv, moved_top):
    rows = lax.broadcasted_iota(jnp.int32, (NB, NB), 0)
    lanes = lax.broadcasted_iota(jnp.int32, (NB, NB), 1)
    upper = jnp.where(rows <= lanes, inv, 0.0)
    lower = jnp.where(rows > lanes, inv, jnp.where(rows == lanes, 1.0, 0.0))
    urows = jnp.dot(lower, moved_top, precision=lax.Precision.HIGHEST, preferred_element_type=F32)
    return upper, urows


def finish_kernel(piv_s, held, fix, out, rows_s, store_sem, row_sem):
    blocks = store_sem.shape[0]
    size = held.shape[0] // blocks
    px = lax.axis_index("prow")
    stores = []
    for b in range(blocks):
        part = pl.ds(b * size, size)
        stores.append(pltpu.make_async_copy(held.at[part], out.at[part], store_sem.at[b]))
    for store in stores:
        store.start()

    def note(j, count):
        target = piv_s[j]
        place = lax.div(target, NB)
        mine = jnp.logical_and(lax.rem(place, SIDE) == px, place > 0)
        rows_s[0, count] = lax.div(place, SIDE) * NB + lax.rem(target, NB)
        rows_s[1, count] = j
        return count + jnp.where(mine, 1, 0)

    count = lax.fori_loop(0, NB, note, jnp.int32(0), unroll=8)
    for store in stores:
        store.wait()

    def row_copy(i):
        here, there = rows_s[1, i], rows_s[0, i]
        return pltpu.make_async_copy(fix.at[pl.ds(here, 1)], out.at[pl.ds(there, 1)], row_sem)

    def start(i, carry):
        row_copy(i).start()
        return carry

    def finish(i, carry):
        row_copy(0).wait()
        return carry

    lax.fori_loop(0, count, start, 0)
    lax.fori_loop(0, count, finish, 0)


def local(matrix, pivots):
    rows_local = matrix.shape[0] * matrix.shape[2]
    held = matrix.reshape(rows_local, NB)
    chunks = rows_local // CHUNK
    smem = pl.BlockSpec(memory_space=pltpu.SMEM)
    vmem = pl.BlockSpec(memory_space=pltpu.VMEM)
    hbm = pl.BlockSpec(memory_space=pl.ANY)
    square = pltpu.VMEM((NB, NB), F32)
    dma = pltpu.SemaphoreType.DMA
    changed, fix = pl.pallas_call(
        exchange_kernel,
        out_shape=(
            jax.ShapeDtypeStruct((rows_local, NB), F32),
            jax.ShapeDtypeStruct((NB, NB), F32),
        ),
        in_specs=[pl.BlockSpec(memory_space=pltpu.HBM), hbm],
        out_specs=(vmem,) * 2,
        scratch_shapes=[
            pltpu.VMEM((rows_local, NB), F32),
            pltpu.VMEM((2 * NB, NB), F32),
            pltpu.VMEM((SIDE, 2 * NB, NB), F32),
            pltpu.VMEM((SIDE, 2 * NB, NB), F32),
            pltpu.VMEM((2 * NB, NB), F32),
            square,
            square,
            square,
            square,
            pltpu.VMEM((2 * NB, 2 * NB), BF16),
            pltpu.VMEM((2 * NB, 2 * NB), BF16),
            pltpu.VMEM((8, NB), jnp.int32),
            pltpu.SMEM((8, NB), jnp.int32),
            pltpu.VMEM((1, NB), jnp.int32),
            pltpu.SMEM((1, NB), jnp.int32),
            dma((2,)),
            dma,
            dma((PIECES * TREES,)),
            dma,
            dma((chunks,)),
            dma((TREES * 4,)),
            dma((TREES,)),
            dma((SIDE - 1,)),
            dma((SIDE,)),
            dma((SIDE,)),
            dma((SIDE,)),
            dma((6,)),
            dma((6,)),
            dma((2,)),
            dma((3,)),
            dma((3,)),
        ],
        compiler_params=pltpu.CompilerParams(
            collective_id=0, has_side_effects=True, vmem_limit_bytes=VMEM_MIB * 2**20
        ),
    )(pltpu.with_memory_space_constraint(pivots.reshape(1, NB), pltpu.HBM), held)
    out = pl.pallas_call(
        finish_kernel,
        out_shape=jax.ShapeDtypeStruct((rows_local, NB), F32),
        in_specs=[smem, vmem, vmem],
        out_specs=hbm,
        scratch_shapes=[pltpu.SMEM((2, 2 * NB), jnp.int32), dma((4,)), dma],
        compiler_params=pltpu.CompilerParams(vmem_limit_bytes=4 * 2**20),
    )(pivots, changed, fix)
    return out.reshape(matrix.shape)


def solution(mesh):
    return jax.shard_map(
        local,
        mesh=mesh,
        in_specs=(P(None, "prow", None, None, "pcol", None), P()),
        out_specs=P(None, "prow", None, None, "pcol", None),
        check_vma=False,
    )
```

```python
import functools

import jax
import jax.numpy as jnp
from jax import lax
from jax.experimental import pallas as pl
from jax.experimental.pallas import tpu as pltpu
from jax.sharding import PartitionSpec as P

MESH = pl.DeviceIdType.MESH
F32 = jnp.float32
BF16 = jnp.bfloat16
NB = 128
SIDE = 4
TREES = 4
STEPS = ((1, 0), (-1, 0), (0, 1), (0, -1))
SENDERS = (
    ((0, 4, 8, 9, 10, 11), (5, 6, 7), (4, 5, 8, 9), (4, 8)),
    ((13, 14, 15), (0, 8, 9, 10, 11, 12, 13, 14, 15), (12, 13), (12,)),
    ((1, 2, 5, 6), (1, 2), (0, 1, 2, 6, 10, 14), (5, 9, 13)),
    ((3, 7), (3,), (7, 11, 15), (0, 2, 3, 6, 7, 10, 11, 14, 15)),
)
PLAIN, ROUND = 5, 6
CHUNK = 128
PIECES = 4
EARLY = 24
LOW_AT = 16
READY = 39
FASTER = 47
WIDE = 4
VMEM_MIB = 40


def one_of(value, places):
    found = value < 0
    for place in places:
        found = jnp.logical_or(found, value == place)
    return found


def lags(tree):
    lag = {0: 0}
    while len(lag) < SIDE * SIDE:
        for d, places in enumerate(SENDERS[tree]):
            for place in places:
                if place in lag:
                    y, z = place // SIDE + STEPS[d][0], place % SIDE + STEPS[d][1]
                    plain = 0 <= y < SIDE and 0 <= z < SIDE
                    lag[y % SIDE * SIDE + z % SIDE] = lag[place] + (PLAIN if plain else ROUND)
    return [lag[place] for place in range(SIDE * SIDE)]


def eliminate_and_invert(a_ref, inv_ref):
    n, b = NB, 8
    lanes1 = lax.broadcasted_iota(jnp.int32, (1, n), 1)
    lanes8 = lax.broadcasted_iota(jnp.int32, (b, n), 1)
    subl = lax.broadcasted_iota(jnp.int32, (b, n), 0)
    rows = lax.broadcasted_iota(jnp.int32, (n, n), 0)
    lanes = lax.broadcasted_iota(jnp.int32, (n, n), 1)
    inv_ref[...] = jnp.zeros((n, n), F32)

    def block(k, carry):
        c0 = pl.multiple_of(k * b, b)

        def pick(x, j):
            return jnp.take_along_axis(x, jnp.full(x.shape, c0 + j, jnp.int32), axis=1)

        row = a_ref[pl.ds(c0, b), :]
        irow = inv_ref[pl.ds(c0, b), :]
        cols = [pick(row, j) for j in range(b)]
        recs, us, prow, pinv, gs = [], {}, [], [], []
        for s in range(b):
            r = 1.0 / jnp.broadcast_to(cols[s][s : s + 1], (b, n))
            recs.append(r[0:1])
            g = jnp.where(subl > s, cols[s] * r, 0.0)
            gs.append(g)
            for j in range(s + 1, b):
                us[s, j] = cols[j][s : s + 1]
                cols[j] = cols[j] - g * us[s, j]
            ar = jnp.where(lanes1 > c0 + s, row[s : s + 1], 0.0)
            row = row - g * ar
            ir = jnp.where(lanes1 == c0 + s, 1.0, irow[s : s + 1])
            irow = irow - g * ir
            prow.append(ar)
            pinv.append(ir)
        for s in range(b):
            row = jnp.where((lanes8 == c0 + s) & (subl > s), gs[s], row)
        whole = a_ref[...]
        inverse = inv_ref[...]
        below = rows >= c0 + b
        own = jnp.where(rows == lanes, 1.0, 0.0)
        mix = jnp.where(below, whole, jnp.where(rows < c0, inverse, own))
        mult = []
        for j in range(b):
            c = pick(mix, j)
            for s in range(j):
                c = c - mult[s] * us[s, j]
            mult.append(c * recs[j])
        upd = whole
        iupd = jnp.where((rows >= c0) & (rows < c0 + b), 0.0, inverse)
        for s in range(b):
            upd = upd - mult[s] * prow[s]
            iupd = iupd - mult[s] * jnp.where(below, pinv[s], prow[s])
        for s in range(b):
            at = lanes == c0 + s
            upd = jnp.where(at, mult[s], upd)
            iupd = jnp.where(at & jnp.logical_not(below), mult[s], iupd)
        a_ref[...] = jnp.where(below, upd, whole)
        inv_ref[...] = iupd
        a_ref[pl.ds(c0, b), :] = row
        inv_ref[pl.ds(c0, b), :] = jnp.where(lanes8 < c0 + subl, irow, inv_ref[pl.ds(c0, b), :])
        return carry

    lax.fori_loop(0, n // b, block, 0)


def exchange_kernel(
    pivots, mat, held, fix,
    panel, contrib, xbuf, dbuf, moved, diag, low_rows, inv, packed, solved, right_upper, right_rows, src_v, src_s, piv_v, piv_s,
    pivot_sem, load_sem, piece_sem, src_sem, recv_sem, tree_sem, part_sem, x_send, x_recv, d_send, d_recv,
    z_send, y_send, f_recv, c_send, c_recv, low_tree, low_part, low_recv,
):
    rows_local = held.shape[0]
    share = rows_local // TREES
    chunks = share // CHUNK
    per_piece = chunks // PIECES
    piece_rows = per_piece * CHUNK
    px = lax.axis_index("prow")
    pc = lax.axis_index("pcol")
    core = lax.rem(pc, 2)
    chip = lax.div(pc, 2)
    y = lax.div(chip, SIDE)
    z = lax.rem(chip, SIDE)
    is_root = pc == 0
    is_root1 = pc == 1
    partner = (px, pc + 1 - 2 * core)

    def pcol_of(yy, zz):
        return (lax.rem(yy + SIDE, SIDE) * SIDE + lax.rem(zz + SIDE, SIDE)) * 2 + core

    x_peers = [(lax.rem(px + k, SIDE), pc) for k in range(1, SIDE)]
    y_peers = [(px, pcol_of(y + k, z)) for k in range(1, SIDE)]
    z_peers = [(px, pcol_of(y, z + k)) for k in range(1, SIDE)]
    cross = [(lax.rem(px + k, SIDE), 1 - pc) for k in range(1, SIDE)]

    def remote(src, dst, send, recv, where):
        return pltpu.make_async_remote_copy(
            src_ref=src, dst_ref=dst, send_sem=send, recv_sem=recv, device_id=where, device_id_type=MESH
        )

    pivot_copies = [
        pltpu.make_async_copy(pivots, piv_s, pivot_sem.at[0]),
        pltpu.make_async_copy(pivots, piv_v, pivot_sem.at[1]),
    ]
    for copy in pivot_copies:
        copy.start()

    hold = pltpu.make_async_copy(mat, held, load_sem)
    pieces = []
    for q in range(PIECES):
        for t in range(TREES):
            part = pl.ds(t * share + q * piece_rows, piece_rows)
            pieces.append(pltpu.make_async_copy(mat.at[part], panel.at[part], piece_sem.at[q * TREES + t]))

    @pl.when(is_root)
    def _():
        for piece in pieces:
            piece.start()

    @pl.when(jnp.logical_not(is_root))
    def _():
        hold.start()

    barrier = pltpu.get_barrier_semaphore()
    for where in x_peers + y_peers + z_peers + [partner]:
        pl.semaphore_signal(barrier, inc=1, device_id=where, device_id_type=MESH)

    @pl.when(pc < 2)
    def _():
        for where in cross:
            pl.semaphore_signal(barrier, inc=1, device_id=where, device_id_type=MESH)

    to_scalars = pltpu.make_async_copy(src_v, src_s, src_sem)

    def find_sources():
        for copy in pivot_copies:
            copy.wait()
        which = lax.broadcasted_iota(jnp.int32, (8, NB), 0)
        sources = jnp.where(which == 0, lax.broadcasted_iota(jnp.int32, (8, NB), 1), piv_v[...])

        def back(step, sources):
            column = NB - 1 - step
            other = piv_s[0, column]
            return jnp.where(sources == column, other, jnp.where(sources == other, column, sources))

        src_v[...] = lax.fori_loop(0, NB, back, sources, unroll=8)
        to_scalars.start()

    @pl.when(jnp.logical_not(is_root))
    def _():
        find_sources()

    @pl.when(pc < 2)
    def _():
        pl.semaphore_wait(barrier, 13)

    @pl.when(pc >= 2)
    def _():
        pl.semaphore_wait(barrier, 10)

    feeds, delay = [], []
    targets = [(px, pcol_of(y + dy, z + dz)) for dy, dz in STEPS]
    for t in range(TREES):
        feeds.append([one_of(chip, SENDERS[t][d]) for d in range(4)])
        late = 0
        for place, lag in enumerate(lags(t)):
            late = late + jnp.where(chip == place, lag, 0)
        delay.append(late)

    def chunk_at(t, c):
        return panel.at[pl.ds(pl.multiple_of(t * share + c * CHUNK, CHUNK), CHUNK)]

    def forward(t, c):
        block = chunk_at(t, c)
        arrival = recv_sem.at[t * chunks + c]
        for d in range(4):

            @pl.when(feeds[t][d])
            def _():
                remote(block, block, tree_sem.at[t * 4 + d], arrival, targets[d]).start()

        remote(block, block, part_sem.at[t], arrival, partner).start()

    def low_piece(t):
        return low_rows.at[pl.ds(t * (NB // TREES), NB // TREES)]

    def forward_low(t):
        low = low_piece(t)
        for d in range(4):

            @pl.when(feeds[t][d])
            def _():
                remote(low, low, low_tree.at[t * 4 + d], low_recv.at[t], targets[d]).start()

        remote(low, low, low_part.at[t], low_recv.at[t], partner).start()

    def forward_range(lo, hi):
        def one(c, carry):
            for t in range(TREES):
                forward(t, c)
            return carry

        lax.fori_loop(lo, hi, one, 0)

    @pl.when(is_root)
    def _():
        for piece in pieces[:TREES]:
            piece.wait()
        forward_range(0, per_piece)
        find_sources()

    to_scalars.wait()

    def gather_from(rows_ref):
        def gather(g, carry):
            for r in range(2):
                base = pl.multiple_of(g * 8, 8)
                found = []
                for s in range(8):
                    source = src_s[r, g * 8 + s]
                    block = lax.div(source, NB)
                    mine = lax.rem(block, SIDE) == px
                    local = lax.div(block, SIDE) * NB + lax.rem(source, NB)
                    row = rows_ref[pl.ds(jnp.where(mine, local, 0), 1), :]
                    found.append(jnp.where(mine, row, 0.0))
                contrib[pl.ds(r * NB + base, 8), :] = jnp.concatenate(found, axis=0)
            return carry

        lax.fori_loop(0, NB // 8, gather, 0)

    @pl.when(is_root)
    def _():
        for piece in pieces[TREES:]:
            piece.wait()
        gather_from(panel)

    @pl.when(jnp.logical_not(is_root))
    def _():
        hold.wait()
        gather_from(held)

    d_copies = []
    for k in range(SIDE):
        where = (lax.rem(px + k, SIDE), pc + 1)
        d_copies.append(remote(contrib.at[pl.ds(0, NB)], dbuf.at[px], d_send.at[k], d_recv.at[px], where))

    @pl.when(is_root)
    def _():
        for copy in d_copies:
            copy.start()

    x_copies = [
        remote(contrib, xbuf.at[px], x_send.at[k], x_recv.at[px], x_peers[k]) for k in range(SIDE - 1)
    ]
    for copy in x_copies:
        copy.start()

    def arrived(ref, sem):
        pltpu.make_async_copy(ref, ref, sem).wait()

    def receive_moved():
        total = contrib[...]
        for k in range(1, SIDE):
            slot = lax.rem(px + k, SIDE)
            arrived(xbuf.at[slot], x_recv.at[slot])
            total = total + xbuf[slot]
        moved[...] = total

    def take_factors():
        upper, urows = factors(inv[...], moved[pl.ds(0, NB), :])
        right_upper[...] = right_side(upper)
        right_rows[...] = right_side(urows)
        solved[...] = urows

    def make_fix():
        low = product(low_rows[...], right_upper[...])
        fix[...] = jnp.where(is_root, low, moved[pl.ds(NB, NB), :] - product(low, right_rows[...]))

    def update(starts, size):
        places = [pl.ds(pl.multiple_of(start, CHUNK), size) for start in starts]
        old = [held[place, :] for place in places]
        upper, rows = right_upper[...], right_rows[...]
        lows = [product(panel[place, :], upper) for place in places]
        for place, x, low in zip(places, old, lows):
            held[place, :] = jnp.where(is_root, low, x - product(low, rows))

    def update_group(g, width):
        update([t * share + g * CHUNK for t in range(TREES)], width * CHUNK)

    def update_rest(lo, hi):
        def one(m, carry):
            update_group(m * WIDE, WIDE)
            return carry

        lax.fori_loop(lax.div(lo, WIDE), hi // WIDE, one, 0)

    @pl.when(is_root)
    def _():
        low_at = min(LOW_AT, chunks - 1)
        forward_range(per_piece, low_at)
        receive_moved()
        low_rows[...] = moved[pl.ds(NB, NB), :]
        for t in range(TREES):
            forward_low(t)
        forward_range(low_at, chunks)
        arrived(packed, c_recv.at[0])
        arrived(inv, c_recv.at[1])
        take_factors()
        make_fix()
        update_rest(jnp.int32(0), chunks)

    assert (FASTER - READY) % WIDE == 0 and READY >= max(max(lags(t)) for t in range(TREES))
    slow = min(FASTER - READY, chunks)
    last = functools.reduce(jnp.maximum, delay) + chunks
    pairs = lax.div(jnp.clip(last - FASTER, 0, (chunks - slow) // 2) + 1, 2) * 2
    done = slow + 2 * pairs

    @pl.when(jnp.logical_and(core == 0, jnp.logical_not(is_root)))
    def _():
        def relay(i, carry):
            for t in range(TREES):
                c = i - delay[t]

                @pl.when(c == min(LOW_AT, chunks - 1))
                def _():
                    arrived(low_piece(t), low_recv.at[t])
                    forward_low(t)

                @pl.when(jnp.logical_and(c >= 0, c < chunks))
                def _():
                    arrived(chunk_at(t, c), recv_sem.at[t * chunks + c])
                    forward(t, c)

            return carry

        def relay_and_one(i, carry):
            relay(i, carry)
            update_group(i - READY, 1)
            return carry

        def relay_and_two(i, carry):
            relay(i, carry)
            update_group(slow + (i - FASTER) * 2, 2)
            return carry

        lax.fori_loop(0, EARLY, relay, 0)
        receive_moved()
        lax.fori_loop(EARLY, READY, relay, 0)
        arrived(packed, c_recv.at[0])
        arrived(inv, c_recv.at[1])
        take_factors()
        lax.fori_loop(READY, FASTER, relay_and_one, 0)
        make_fix()
        lax.fori_loop(FASTER, FASTER + pairs, relay_and_two, 0)
        update_rest(done, chunks)

    z_copies = [remote(diag, diag, z_send.at[k], f_recv, z_peers[k]) for k in range(3)]
    y_copies = [remote(diag, diag, y_send.at[k], f_recv, y_peers[k]) for k in range(3)]
    c_copies = [
        remote(packed, packed, c_send.at[0], c_recv.at[0], partner),
        remote(inv, inv, c_send.at[1], c_recv.at[1], partner),
    ]

    @pl.when(core == 1)
    def _():
        @pl.when(is_root1)
        def _():
            for k in range(SIDE):
                arrived(dbuf.at[k], d_recv.at[k])
            diag[...] = dbuf[0] + dbuf[1] + dbuf[2] + dbuf[3]
            for k in range(3):
                z_copies[k].start()
            for k in range(3):
                y_copies[k].start()

        @pl.when(jnp.logical_not(is_root1))
        def _():
            arrived(diag, f_recv)

            @pl.when(y == 0)
            def _():
                for k in range(3):
                    y_copies[k].start()

        packed[...] = diag[...]
        eliminate_and_invert(packed, inv)
        c_copies[1].start()
        c_copies[0].start()
        receive_moved()
        take_factors()

        def receive(m, carry):
            for i in (2 * m, 2 * m + 1):
                for t in range(TREES):
                    arrived(chunk_at(t, i), recv_sem.at[t * chunks + i])
            update_group(2 * m, 2)
            return carry

        late = chunks // 2 - chunks // 8
        lax.fori_loop(0, late, receive, 0)
        for t in range(TREES):
            arrived(low_piece(t), low_recv.at[t])
        make_fix()
        lax.fori_loop(late, chunks // 2, receive, 0)

        for copy in c_copies:
            copy.wait_send()

        @pl.when(is_root1)
        def _():
            for copy in z_copies:
                copy.wait_send()

        @pl.when(y == 0)
        def _():
            for copy in y_copies:
                copy.wait_send()

    @pl.when(core == 0)
    def _():
        for t in range(TREES):
            sent = panel.at[pl.ds(t * share, share)]
            for d in range(4):

                @pl.when(feeds[t][d])
                def _():
                    remote(sent, sent, tree_sem.at[t * 4 + d], recv_sem.at[0], partner).wait_send()

            remote(sent, sent, part_sem.at[t], recv_sem.at[0], partner).wait_send()
            low = low_piece(t)
            for d in range(4):

                @pl.when(feeds[t][d])
                def _():
                    remote(low, low, low_tree.at[t * 4 + d], low_recv.at[t], partner).wait_send()

            remote(low, low, low_part.at[t], low_recv.at[t], partner).wait_send()

        @pl.when(is_root)
        def _():
            for copy in d_copies:
                copy.wait_send()

    @pl.when(px == 0)
    def _():
        held[pl.ds(0, NB), :] = jnp.where(is_root, packed[...], solved[...])

    for copy in x_copies:
        copy.wait_send()


def split(x):
    high = x.astype(BF16)
    return high, (x - high.astype(F32)).astype(BF16)


def right_side(x):
    high, low = split(x)
    return jnp.concatenate(
        [jnp.concatenate([high, low], axis=1), jnp.concatenate([high, jnp.zeros_like(low)], axis=1)], axis=0
    )


def product(x, right):
    high, low = split(x)
    both = jnp.dot(jnp.concatenate([high, low], axis=1), right, preferred_element_type=F32)
    return both[:, :NB] + both[:, NB:]


def factors(inv, moved_top):
    rows = lax.broadcasted_iota(jnp.int32, (NB, NB), 0)
    lanes = lax.broadcasted_iota(jnp.int32, (NB, NB), 1)
    upper = jnp.where(rows <= lanes, inv, 0.0)
    lower = jnp.where(rows > lanes, inv, jnp.where(rows == lanes, 1.0, 0.0))
    urows = jnp.dot(lower, moved_top, precision=lax.Precision.HIGHEST, preferred_element_type=F32)
    return upper, urows


def finish_kernel(piv_s, held, fix, out, rows_s, store_sem, row_sem):
    blocks = store_sem.shape[0]
    size = held.shape[0] // blocks
    px = lax.axis_index("prow")
    stores = []
    for b in range(blocks):
        part = pl.ds(b * size, size)
        stores.append(pltpu.make_async_copy(held.at[part], out.at[part], store_sem.at[b]))
    for store in stores:
        store.start()

    def note(j, count):
        target = piv_s[j]
        place = lax.div(target, NB)
        mine = jnp.logical_and(lax.rem(place, SIDE) == px, place > 0)
        rows_s[0, count] = lax.div(place, SIDE) * NB + lax.rem(target, NB)
        rows_s[1, count] = j
        return count + jnp.where(mine, 1, 0)

    count = lax.fori_loop(0, NB, note, jnp.int32(0), unroll=8)
    for store in stores:
        store.wait()

    def row_copy(i):
        here, there = rows_s[1, i], rows_s[0, i]
        return pltpu.make_async_copy(fix.at[pl.ds(here, 1)], out.at[pl.ds(there, 1)], row_sem)

    def start(i, carry):
        row_copy(i).start()
        return carry

    def finish(i, carry):
        row_copy(0).wait()
        return carry

    lax.fori_loop(0, count, start, 0)
    lax.fori_loop(0, count, finish, 0)


def local(matrix, pivots):
    rows_local = matrix.shape[0] * matrix.shape[2]
    held = matrix.reshape(rows_local, NB)
    chunks = rows_local // CHUNK
    smem = pl.BlockSpec(memory_space=pltpu.SMEM)
    vmem = pl.BlockSpec(memory_space=pltpu.VMEM)
    hbm = pl.BlockSpec(memory_space=pl.ANY)
    square = pltpu.VMEM((NB, NB), F32)
    dma = pltpu.SemaphoreType.DMA
    changed, fix = pl.pallas_call(
        exchange_kernel,
        out_shape=(
            jax.ShapeDtypeStruct((rows_local, NB), F32),
            jax.ShapeDtypeStruct((NB, NB), F32),
        ),
        in_specs=[pl.BlockSpec(memory_space=pltpu.HBM), hbm],
        out_specs=(vmem,) * 2,
        scratch_shapes=[
            pltpu.VMEM((rows_local, NB), F32),
            pltpu.VMEM((2 * NB, NB), F32),
            pltpu.VMEM((SIDE, 2 * NB, NB), F32),
            pltpu.VMEM((SIDE, NB, NB), F32),
            pltpu.VMEM((2 * NB, NB), F32),
            square,
            square,
            square,
            square,
            square,
            pltpu.VMEM((2 * NB, 2 * NB), BF16),
            pltpu.VMEM((2 * NB, 2 * NB), BF16),
            pltpu.VMEM((8, NB), jnp.int32),
            pltpu.SMEM((8, NB), jnp.int32),
            pltpu.VMEM((1, NB), jnp.int32),
            pltpu.SMEM((1, NB), jnp.int32),
            dma((2,)),
            dma,
            dma((PIECES * TREES,)),
            dma,
            dma((chunks,)),
            dma((TREES * 4,)),
            dma((TREES,)),
            dma((SIDE - 1,)),
            dma((SIDE,)),
            dma((SIDE,)),
            dma((SIDE,)),
            dma((3,)),
            dma((3,)),
            dma,
            dma((2,)),
            dma((2,)),
            dma((TREES * 4,)),
            dma((TREES,)),
            dma((TREES,)),
        ],
        compiler_params=pltpu.CompilerParams(
            collective_id=0, has_side_effects=True, vmem_limit_bytes=VMEM_MIB * 2**20
        ),
    )(pltpu.with_memory_space_constraint(pivots.reshape(1, NB), pltpu.HBM), held)
    out = pl.pallas_call(
        finish_kernel,
        out_shape=jax.ShapeDtypeStruct((rows_local, NB), F32),
        in_specs=[smem, vmem, vmem],
        out_specs=hbm,
        scratch_shapes=[pltpu.SMEM((2, 2 * NB), jnp.int32), dma((4,)), dma],
        compiler_params=pltpu.CompilerParams(vmem_limit_bytes=4 * 2**20),
    )(pivots, changed, fix)
    return out.reshape(matrix.shape)


def solution(mesh):
    return jax.shard_map(
        local,
        mesh=mesh,
        in_specs=(P(None, "prow", None, None, "pcol", None), P()),
        out_specs=P(None, "prow", None, None, "pcol", None),
        check_vma=False,
    )
```

```python
import functools

import jax
import jax.numpy as jnp
from jax import lax
from jax.experimental import pallas as pl
from jax.experimental.pallas import tpu as pltpu
from jax.sharding import PartitionSpec as P

MESH = pl.DeviceIdType.MESH
F32 = jnp.float32
BF16 = jnp.bfloat16
NB = 128
SIDE = 4
TREES = 4
STEPS = ((1, 0), (-1, 0), (0, 1), (0, -1))
SENDERS = (
    ((0, 4, 8, 9, 10, 11), (5, 6, 7), (4, 5, 8, 9), (4, 8)),
    ((13, 14, 15), (0, 8, 9, 10, 11, 12, 13, 14, 15), (12, 13), (12,)),
    ((1, 2, 5, 6), (1, 2), (0, 1, 2, 6, 10, 14), (5, 9, 13)),
    ((3, 7), (3,), (7, 11, 15), (0, 2, 3, 6, 7, 10, 11, 14, 15)),
)
PLAIN, ROUND = 5, 6
CHUNK = 128
PIECES = 4
EARLY = 30
LOW_AT = 16
READY = 39
FASTER = 47
WIDE = 4
VMEM_MIB = 40


def one_of(value, places):
    found = value < 0
    for place in places:
        found = jnp.logical_or(found, value == place)
    return found


def lags(tree):
    lag = {0: 0}
    while len(lag) < SIDE * SIDE:
        for d, places in enumerate(SENDERS[tree]):
            for place in places:
                if place in lag:
                    y, z = place // SIDE + STEPS[d][0], place % SIDE + STEPS[d][1]
                    plain = 0 <= y < SIDE and 0 <= z < SIDE
                    lag[y % SIDE * SIDE + z % SIDE] = lag[place] + (PLAIN if plain else ROUND)
    return [lag[place] for place in range(SIDE * SIDE)]


def eliminate_and_invert(a_ref, inv_ref):
    n, b = NB, 8
    lanes1 = lax.broadcasted_iota(jnp.int32, (1, n), 1)
    lanes8 = lax.broadcasted_iota(jnp.int32, (b, n), 1)
    subl = lax.broadcasted_iota(jnp.int32, (b, n), 0)
    rows = lax.broadcasted_iota(jnp.int32, (n, n), 0)
    lanes = lax.broadcasted_iota(jnp.int32, (n, n), 1)
    inv_ref[...] = jnp.zeros((n, n), F32)

    def block(k, carry):
        c0 = pl.multiple_of(k * b, b)

        def pick(x, j):
            return jnp.take_along_axis(x, jnp.full(x.shape, c0 + j, jnp.int32), axis=1)

        row = a_ref[pl.ds(c0, b), :]
        irow = inv_ref[pl.ds(c0, b), :]
        cols = [pick(row, j) for j in range(b)]
        recs, us, prow, pinv, gs = [], {}, [], [], []
        for s in range(b):
            r = 1.0 / jnp.broadcast_to(cols[s][s : s + 1], (b, n))
            recs.append(r[0:1])
            g = jnp.where(subl > s, cols[s] * r, 0.0)
            gs.append(g)
            for j in range(s + 1, b):
                us[s, j] = cols[j][s : s + 1]
                cols[j] = cols[j] - g * us[s, j]
            ar = jnp.where(lanes1 > c0 + s, row[s : s + 1], 0.0)
            row = row - g * ar
            ir = jnp.where(lanes1 == c0 + s, 1.0, irow[s : s + 1])
            irow = irow - g * ir
            prow.append(ar)
            pinv.append(ir)
        for s in range(b):
            row = jnp.where((lanes8 == c0 + s) & (subl > s), gs[s], row)
        whole = a_ref[...]
        inverse = inv_ref[...]
        below = rows >= c0 + b
        own = jnp.where(rows == lanes, 1.0, 0.0)
        mix = jnp.where(below, whole, jnp.where(rows < c0, inverse, own))
        mult = []
        for j in range(b):
            c = pick(mix, j)
            for s in range(j):
                c = c - mult[s] * us[s, j]
            mult.append(c * recs[j])
        upd = whole
        iupd = jnp.where((rows >= c0) & (rows < c0 + b), 0.0, inverse)
        for s in range(b):
            upd = upd - mult[s] * prow[s]
            iupd = iupd - mult[s] * jnp.where(below, pinv[s], prow[s])
        for s in range(b):
            at = lanes == c0 + s
            upd = jnp.where(at, mult[s], upd)
            iupd = jnp.where(at & jnp.logical_not(below), mult[s], iupd)
        a_ref[...] = jnp.where(below, upd, whole)
        inv_ref[...] = iupd
        a_ref[pl.ds(c0, b), :] = row
        inv_ref[pl.ds(c0, b), :] = jnp.where(lanes8 < c0 + subl, irow, inv_ref[pl.ds(c0, b), :])
        return carry

    lax.fori_loop(0, n // b, block, 0)


def exchange_kernel(
    pivots, mat, held, fix,
    panel, contrib, xbuf, dbuf, moved, diag, low_rows, inv, packed, solved, right_upper, right_rows, src_v, src_s, piv_v, piv_s,
    pivot_sem, load_sem, piece_sem, src_sem, recv_sem, tree_sem, part_sem, x_send, x_recv, d_send, d_recv,
    z_send, y_send, f_recv, c_send, c_recv, low_tree, low_part, low_recv,
):
    rows_local = held.shape[0]
    share = rows_local // TREES
    chunks = share // CHUNK
    per_piece = chunks // PIECES
    piece_rows = per_piece * CHUNK
    px = lax.axis_index("prow")
    pc = lax.axis_index("pcol")
    core = lax.rem(pc, 2)
    chip = lax.div(pc, 2)
    y = lax.div(chip, SIDE)
    z = lax.rem(chip, SIDE)
    is_root = pc == 0
    is_root1 = pc == 1
    partner = (px, pc + 1 - 2 * core)

    def pcol_of(yy, zz):
        return (lax.rem(yy + SIDE, SIDE) * SIDE + lax.rem(zz + SIDE, SIDE)) * 2 + core

    x_peers = [(lax.rem(px + k, SIDE), pc) for k in range(1, SIDE)]
    y_peers = [(px, pcol_of(y + k, z)) for k in range(1, SIDE)]
    z_peers = [(px, pcol_of(y, z + k)) for k in range(1, SIDE)]
    cross = [(lax.rem(px + k, SIDE), 1 - pc) for k in range(1, SIDE)]

    def remote(src, dst, send, recv, where):
        return pltpu.make_async_remote_copy(
            src_ref=src, dst_ref=dst, send_sem=send, recv_sem=recv, device_id=where, device_id_type=MESH
        )

    pivot_copies = [
        pltpu.make_async_copy(pivots, piv_s, pivot_sem.at[0]),
        pltpu.make_async_copy(pivots, piv_v, pivot_sem.at[1]),
    ]
    for copy in pivot_copies:
        copy.start()

    hold = pltpu.make_async_copy(mat, held, load_sem)
    pieces = []
    for q in range(PIECES):
        for t in range(TREES):
            part = pl.ds(t * share + q * piece_rows, piece_rows)
            pieces.append(pltpu.make_async_copy(mat.at[part], panel.at[part], piece_sem.at[q * TREES + t]))

    @pl.when(is_root)
    def _():
        for piece in pieces:
            piece.start()

    @pl.when(jnp.logical_not(is_root))
    def _():
        hold.start()

    barrier = pltpu.get_barrier_semaphore()
    for where in x_peers + y_peers + z_peers + [partner]:
        pl.semaphore_signal(barrier, inc=1, device_id=where, device_id_type=MESH)

    @pl.when(pc < 2)
    def _():
        for where in cross:
            pl.semaphore_signal(barrier, inc=1, device_id=where, device_id_type=MESH)

    to_scalars = pltpu.make_async_copy(src_v, src_s, src_sem)

    def find_sources():
        for copy in pivot_copies:
            copy.wait()
        which = lax.broadcasted_iota(jnp.int32, (8, NB), 0)
        sources = jnp.where(which == 0, lax.broadcasted_iota(jnp.int32, (8, NB), 1), piv_v[...])

        def back(step, sources):
            column = NB - 1 - step
            other = piv_s[0, column]
            return jnp.where(sources == column, other, jnp.where(sources == other, column, sources))

        src_v[...] = lax.fori_loop(0, NB, back, sources, unroll=8)
        to_scalars.start()

    @pl.when(jnp.logical_not(is_root))
    def _():
        find_sources()

    @pl.when(pc < 2)
    def _():
        pl.semaphore_wait(barrier, 13)

    @pl.when(pc >= 2)
    def _():
        pl.semaphore_wait(barrier, 10)

    feeds, delay = [], []
    targets = [(px, pcol_of(y + dy, z + dz)) for dy, dz in STEPS]
    for t in range(TREES):
        feeds.append([one_of(chip, SENDERS[t][d]) for d in range(4)])
        late = 0
        for place, lag in enumerate(lags(t)):
            late = late + jnp.where(chip == place, lag, 0)
        delay.append(late)

    def chunk_at(t, c):
        return panel.at[pl.ds(pl.multiple_of(t * share + c * CHUNK, CHUNK), CHUNK)]

    def forward(t, c):
        block = chunk_at(t, c)
        arrival = recv_sem.at[t * chunks + c]
        for d in range(4):

            @pl.when(feeds[t][d])
            def _():
                remote(block, block, tree_sem.at[t * 4 + d], arrival, targets[d]).start()

        remote(block, block, part_sem.at[t], arrival, partner).start()

    def low_piece(t):
        return low_rows.at[pl.ds(t * (NB // TREES), NB // TREES)]

    def forward_low(t):
        low = low_piece(t)
        for d in range(4):

            @pl.when(feeds[t][d])
            def _():
                remote(low, low, low_tree.at[t * 4 + d], low_recv.at[t], targets[d]).start()

        remote(low, low, low_part.at[t], low_recv.at[t], partner).start()

    def forward_range(lo, hi):
        def one(c, carry):
            for t in range(TREES):
                forward(t, c)
            return carry

        lax.fori_loop(lo, hi, one, 0)

    @pl.when(is_root)
    def _():
        for piece in pieces[:TREES]:
            piece.wait()
        forward_range(0, per_piece)
        find_sources()

    to_scalars.wait()

    def gather(g, rows_ref):
        for r in range(2):
            base = pl.multiple_of(g * 8, 8)
            found = []
            for s in range(8):
                source = src_s[r, g * 8 + s]
                block = lax.div(source, NB)
                mine = lax.rem(block, SIDE) == px
                local = lax.div(block, SIDE) * NB + lax.rem(source, NB)
                row = rows_ref[pl.ds(jnp.where(mine, local, 0), 1), :]
                found.append(jnp.where(mine, row, 0.0))
            contrib[pl.ds(r * NB + base, 8), :] = jnp.concatenate(found, axis=0)

    def gather_from(rows_ref):
        def one(g, carry):
            gather(g, rows_ref)
            return carry

        lax.fori_loop(0, NB // 8, one, 0)

    @pl.when(is_root)
    def _():
        for piece in pieces[TREES:]:
            piece.wait()
        gather_from(panel)

    @pl.when(jnp.logical_not(is_root))
    def _():
        hold.wait()

        @pl.when(core == 1)
        def _():
            gather_from(held)

    d_copies = []
    for k in range(SIDE):
        where = (lax.rem(px + k, SIDE), pc + 1)
        d_copies.append(remote(contrib.at[pl.ds(0, NB)], dbuf.at[px], d_send.at[k], d_recv.at[px], where))

    @pl.when(is_root)
    def _():
        for copy in d_copies:
            copy.start()

    x_copies = [
        remote(contrib, xbuf.at[px], x_send.at[k], x_recv.at[px], x_peers[k]) for k in range(SIDE - 1)
    ]

    @pl.when(jnp.logical_or(core == 1, is_root))
    def _():
        for copy in x_copies:
            copy.start()

    def arrived(ref, sem):
        pltpu.make_async_copy(ref, ref, sem).wait()

    def receive_moved():
        total = contrib[...]
        for k in range(1, SIDE):
            slot = lax.rem(px + k, SIDE)
            arrived(xbuf.at[slot], x_recv.at[slot])
            total = total + xbuf[slot]
        moved[...] = total

    def take_factors():
        upper, urows = factors(inv[...], moved[pl.ds(0, NB), :])
        right_upper[...] = right_side(upper)
        right_rows[...] = right_side(urows)
        solved[...] = urows

    def make_fix():
        low = product(low_rows[...], right_upper[...])
        fix[...] = jnp.where(is_root, low, moved[pl.ds(NB, NB), :] - product(low, right_rows[...]))

    def update(starts, size):
        places = [pl.ds(pl.multiple_of(start, CHUNK), size) for start in starts]
        old = [held[place, :] for place in places]
        upper, rows = right_upper[...], right_rows[...]
        lows = [product(panel[place, :], upper) for place in places]
        for place, x, low in zip(places, old, lows):
            held[place, :] = jnp.where(is_root, low, x - product(low, rows))

    def update_group(g, width):
        update([t * share + g * CHUNK for t in range(TREES)], width * CHUNK)

    def update_rest(lo, hi):
        def one(m, carry):
            update_group(m * WIDE, WIDE)
            return carry

        lax.fori_loop(lax.div(lo, WIDE), hi // WIDE, one, 0)

    @pl.when(is_root)
    def _():
        low_at = min(LOW_AT, chunks - 1)
        forward_range(per_piece, low_at)
        receive_moved()
        low_rows[...] = moved[pl.ds(NB, NB), :]
        for t in range(TREES):
            forward_low(t)
        forward_range(low_at, chunks)
        arrived(packed, c_recv.at[0])
        arrived(inv, c_recv.at[1])
        take_factors()
        make_fix()
        update_rest(jnp.int32(0), chunks)

    assert (FASTER - READY) % WIDE == 0 and READY >= max(max(lags(t)) for t in range(TREES))
    slow = min(FASTER - READY, chunks)
    last = functools.reduce(jnp.maximum, delay) + chunks
    pairs = lax.div(jnp.clip(last - FASTER, 0, (chunks - slow) // 2) + 1, 2) * 2
    done = slow + 2 * pairs

    @pl.when(jnp.logical_and(core == 0, jnp.logical_not(is_root)))
    def _():
        def relay(i, carry):
            for t in range(TREES):
                c = i - delay[t]

                @pl.when(c == min(LOW_AT, chunks - 1))
                def _():
                    arrived(low_piece(t), low_recv.at[t])
                    forward_low(t)

                @pl.when(jnp.logical_and(c >= 0, c < chunks))
                def _():
                    arrived(chunk_at(t, c), recv_sem.at[t * chunks + c])
                    forward(t, c)

            return carry

        def relay_and_one(i, carry):
            relay(i, carry)
            update_group(i - READY, 1)
            return carry

        def relay_and_two(i, carry):
            relay(i, carry)
            update_group(slow + (i - FASTER) * 2, 2)
            return carry

        def relay_and_gather(i, carry):
            relay(i, carry)
            gather(i, held)
            return carry

        lax.fori_loop(0, NB // 8, relay_and_gather, 0)
        for copy in x_copies:
            copy.start()
        lax.fori_loop(NB // 8, EARLY, relay, 0)
        receive_moved()
        lax.fori_loop(EARLY, READY, relay, 0)
        arrived(packed, c_recv.at[0])
        arrived(inv, c_recv.at[1])
        take_factors()
        lax.fori_loop(READY, FASTER, relay_and_one, 0)
        make_fix()
        lax.fori_loop(FASTER, FASTER + pairs, relay_and_two, 0)
        update_rest(done, chunks)

    z_copies = [remote(diag, diag, z_send.at[k], f_recv, z_peers[k]) for k in range(3)]
    y_copies = [remote(diag, diag, y_send.at[k], f_recv, y_peers[k]) for k in range(3)]
    c_copies = [
        remote(packed, packed, c_send.at[0], c_recv.at[0], partner),
        remote(inv, inv, c_send.at[1], c_recv.at[1], partner),
    ]

    @pl.when(core == 1)
    def _():
        @pl.when(is_root1)
        def _():
            for k in range(SIDE):
                arrived(dbuf.at[k], d_recv.at[k])
            diag[...] = dbuf[0] + dbuf[1] + dbuf[2] + dbuf[3]
            for k in range(3):
                z_copies[k].start()
            for k in range(3):
                y_copies[k].start()

        @pl.when(jnp.logical_not(is_root1))
        def _():
            arrived(diag, f_recv)

            @pl.when(y == 0)
            def _():
                for k in range(3):
                    y_copies[k].start()

        packed[...] = diag[...]
        eliminate_and_invert(packed, inv)
        c_copies[1].start()
        c_copies[0].start()
        receive_moved()
        take_factors()

        def receive(m, carry):
            for i in (2 * m, 2 * m + 1):
                for t in range(TREES):
                    arrived(chunk_at(t, i), recv_sem.at[t * chunks + i])
            update_group(2 * m, 2)
            return carry

        late = chunks // 2 - chunks // 8
        lax.fori_loop(0, late, receive, 0)
        for t in range(TREES):
            arrived(low_piece(t), low_recv.at[t])
        make_fix()
        lax.fori_loop(late, chunks // 2, receive, 0)

        for copy in c_copies:
            copy.wait_send()

        @pl.when(is_root1)
        def _():
            for copy in z_copies:
                copy.wait_send()

        @pl.when(y == 0)
        def _():
            for copy in y_copies:
                copy.wait_send()

    @pl.when(core == 0)
    def _():
        for t in range(TREES):
            sent = panel.at[pl.ds(t * share, share)]
            for d in range(4):

                @pl.when(feeds[t][d])
                def _():
                    remote(sent, sent, tree_sem.at[t * 4 + d], recv_sem.at[0], partner).wait_send()

            remote(sent, sent, part_sem.at[t], recv_sem.at[0], partner).wait_send()
            low = low_piece(t)
            for d in range(4):

                @pl.when(feeds[t][d])
                def _():
                    remote(low, low, low_tree.at[t * 4 + d], low_recv.at[t], partner).wait_send()

            remote(low, low, low_part.at[t], low_recv.at[t], partner).wait_send()

        @pl.when(is_root)
        def _():
            for copy in d_copies:
                copy.wait_send()

    @pl.when(px == 0)
    def _():
        held[pl.ds(0, NB), :] = jnp.where(is_root, packed[...], solved[...])

    for copy in x_copies:
        copy.wait_send()


def split(x):
    high = x.astype(BF16)
    return high, (x - high.astype(F32)).astype(BF16)


def right_side(x):
    high, low = split(x)
    return jnp.concatenate(
        [jnp.concatenate([high, low], axis=1), jnp.concatenate([high, jnp.zeros_like(low)], axis=1)], axis=0
    )


def product(x, right):
    high, low = split(x)
    both = jnp.dot(jnp.concatenate([high, low], axis=1), right, preferred_element_type=F32)
    return both[:, :NB] + both[:, NB:]


def factors(inv, moved_top):
    rows = lax.broadcasted_iota(jnp.int32, (NB, NB), 0)
    lanes = lax.broadcasted_iota(jnp.int32, (NB, NB), 1)
    upper = jnp.where(rows <= lanes, inv, 0.0)
    lower = jnp.where(rows > lanes, inv, jnp.where(rows == lanes, 1.0, 0.0))
    urows = jnp.dot(lower, moved_top, precision=lax.Precision.HIGHEST, preferred_element_type=F32)
    return upper, urows


def finish_kernel(piv_s, held, fix, out, rows_s, store_sem, row_sem):
    blocks = store_sem.shape[0]
    size = held.shape[0] // blocks
    px = lax.axis_index("prow")
    stores = []
    for b in range(blocks):
        part = pl.ds(b * size, size)
        stores.append(pltpu.make_async_copy(held.at[part], out.at[part], store_sem.at[b]))
    for store in stores:
        store.start()

    def note(j, count):
        target = piv_s[j]
        place = lax.div(target, NB)
        mine = jnp.logical_and(lax.rem(place, SIDE) == px, place > 0)
        rows_s[0, count] = lax.div(place, SIDE) * NB + lax.rem(target, NB)
        rows_s[1, count] = j
        return count + jnp.where(mine, 1, 0)

    count = lax.fori_loop(0, NB, note, jnp.int32(0), unroll=8)
    for store in stores:
        store.wait()

    def row_copy(i):
        here, there = rows_s[1, i], rows_s[0, i]
        return pltpu.make_async_copy(fix.at[pl.ds(here, 1)], out.at[pl.ds(there, 1)], row_sem)

    def start(i, carry):
        row_copy(i).start()
        return carry

    def finish(i, carry):
        row_copy(0).wait()
        return carry

    lax.fori_loop(0, count, start, 0)
    lax.fori_loop(0, count, finish, 0)


def local(matrix, pivots):
    rows_local = matrix.shape[0] * matrix.shape[2]
    held = matrix.reshape(rows_local, NB)
    chunks = rows_local // CHUNK
    smem = pl.BlockSpec(memory_space=pltpu.SMEM)
    vmem = pl.BlockSpec(memory_space=pltpu.VMEM)
    hbm = pl.BlockSpec(memory_space=pl.ANY)
    square = pltpu.VMEM((NB, NB), F32)
    dma = pltpu.SemaphoreType.DMA
    changed, fix = pl.pallas_call(
        exchange_kernel,
        out_shape=(
            jax.ShapeDtypeStruct((rows_local, NB), F32),
            jax.ShapeDtypeStruct((NB, NB), F32),
        ),
        in_specs=[pl.BlockSpec(memory_space=pltpu.HBM), hbm],
        out_specs=(vmem,) * 2,
        scratch_shapes=[
            pltpu.VMEM((rows_local, NB), F32),
            pltpu.VMEM((2 * NB, NB), F32),
            pltpu.VMEM((SIDE, 2 * NB, NB), F32),
            pltpu.VMEM((SIDE, NB, NB), F32),
            pltpu.VMEM((2 * NB, NB), F32),
            square,
            square,
            square,
            square,
            square,
            pltpu.VMEM((2 * NB, 2 * NB), BF16),
            pltpu.VMEM((2 * NB, 2 * NB), BF16),
            pltpu.VMEM((8, NB), jnp.int32),
            pltpu.SMEM((8, NB), jnp.int32),
            pltpu.VMEM((1, NB), jnp.int32),
            pltpu.SMEM((1, NB), jnp.int32),
            dma((2,)),
            dma,
            dma((PIECES * TREES,)),
            dma,
            dma((chunks,)),
            dma((TREES * 4,)),
            dma((TREES,)),
            dma((SIDE - 1,)),
            dma((SIDE,)),
            dma((SIDE,)),
            dma((SIDE,)),
            dma((3,)),
            dma((3,)),
            dma,
            dma((2,)),
            dma((2,)),
            dma((TREES * 4,)),
            dma((TREES,)),
            dma((TREES,)),
        ],
        compiler_params=pltpu.CompilerParams(
            collective_id=0, has_side_effects=True, vmem_limit_bytes=VMEM_MIB * 2**20
        ),
    )(pltpu.with_memory_space_constraint(pivots.reshape(1, NB), pltpu.HBM), held)
    out = pl.pallas_call(
        finish_kernel,
        out_shape=jax.ShapeDtypeStruct((rows_local, NB), F32),
        in_specs=[smem, vmem, vmem],
        out_specs=hbm,
        scratch_shapes=[pltpu.SMEM((2, 2 * NB), jnp.int32), dma((4,)), dma],
        compiler_params=pltpu.CompilerParams(vmem_limit_bytes=4 * 2**20),
    )(pivots, changed, fix)
    return out.reshape(matrix.shape)


def solution(mesh):
    return jax.shard_map(
        local,
        mesh=mesh,
        in_specs=(P(None, "prow", None, None, "pcol", None), P()),
        out_specs=P(None, "prow", None, None, "pcol", None),
        check_vma=False,
    )
```

```python
import functools

import jax
import jax.numpy as jnp
from jax import lax
from jax.experimental import pallas as pl
from jax.experimental.pallas import tpu as pltpu
from jax.sharding import PartitionSpec as P

MESH = pl.DeviceIdType.MESH
F32 = jnp.float32
BF16 = jnp.bfloat16
NB = 128
SIDE = 4
TREES = 4
STEPS = ((1, 0), (-1, 0), (0, 1), (0, -1))
SENDERS = (
    ((0, 4, 8, 9, 10, 11), (5, 6, 7), (4, 5, 8, 9), (4, 8)),
    ((13, 14, 15), (0, 8, 9, 10, 11, 12, 13, 14, 15), (12, 13), (12,)),
    ((1, 2, 5, 6), (1, 2), (0, 1, 2, 6, 10, 14), (5, 9, 13)),
    ((3, 7), (3,), (7, 11, 15), (0, 2, 3, 6, 7, 10, 11, 14, 15)),
)
PLAIN, ROUND = 5, 6
CHUNK = 128
PIECES = 4
EARLY = 32
LOW_AT = 20
READY = 39
FASTER = 47
WIDE = 4
VMEM_MIB = 40


def one_of(value, places):
    found = value < 0
    for place in places:
        found = jnp.logical_or(found, value == place)
    return found


def lags(tree):
    lag = {0: 0}
    while len(lag) < SIDE * SIDE:
        for d, places in enumerate(SENDERS[tree]):
            for place in places:
                if place in lag:
                    y, z = place // SIDE + STEPS[d][0], place % SIDE + STEPS[d][1]
                    plain = 0 <= y < SIDE and 0 <= z < SIDE
                    lag[y % SIDE * SIDE + z % SIDE] = lag[place] + (PLAIN if plain else ROUND)
    return [lag[place] for place in range(SIDE * SIDE)]


def eliminate_and_invert(a_ref, inv_ref):
    n, b = NB, 8
    lanes1 = lax.broadcasted_iota(jnp.int32, (1, n), 1)
    lanes8 = lax.broadcasted_iota(jnp.int32, (b, n), 1)
    subl = lax.broadcasted_iota(jnp.int32, (b, n), 0)
    rows = lax.broadcasted_iota(jnp.int32, (n, n), 0)
    lanes = lax.broadcasted_iota(jnp.int32, (n, n), 1)
    inv_ref[...] = jnp.zeros((n, n), F32)

    def block(k, carry):
        c0 = pl.multiple_of(k * b, b)

        def pick(x, j):
            return jnp.take_along_axis(x, jnp.full(x.shape, c0 + j, jnp.int32), axis=1)

        row = a_ref[pl.ds(c0, b), :]
        irow = inv_ref[pl.ds(c0, b), :]
        cols = [pick(row, j) for j in range(b)]
        recs, us, prow, pinv, gs = [], {}, [], [], []
        for s in range(b):
            r = 1.0 / jnp.broadcast_to(cols[s][s : s + 1], (b, n))
            recs.append(r[0:1])
            g = jnp.where(subl > s, cols[s] * r, 0.0)
            gs.append(g)
            for j in range(s + 1, b):
                us[s, j] = cols[j][s : s + 1]
                cols[j] = cols[j] - g * us[s, j]
            ar = jnp.where(lanes1 > c0 + s, row[s : s + 1], 0.0)
            row = row - g * ar
            ir = jnp.where(lanes1 == c0 + s, 1.0, irow[s : s + 1])
            irow = irow - g * ir
            prow.append(ar)
            pinv.append(ir)
        for s in range(b):
            row = jnp.where((lanes8 == c0 + s) & (subl > s), gs[s], row)
        whole = a_ref[...]
        inverse = inv_ref[...]
        below = rows >= c0 + b
        own = jnp.where(rows == lanes, 1.0, 0.0)
        mix = jnp.where(below, whole, jnp.where(rows < c0, inverse, own))
        mult = []
        for j in range(b):
            c = pick(mix, j)
            for s in range(j):
                c = c - mult[s] * us[s, j]
            mult.append(c * recs[j])
        upd = whole
        iupd = jnp.where((rows >= c0) & (rows < c0 + b), 0.0, inverse)
        for s in range(b):
            upd = upd - mult[s] * prow[s]
            iupd = iupd - mult[s] * jnp.where(below, pinv[s], prow[s])
        for s in range(b):
            at = lanes == c0 + s
            upd = jnp.where(at, mult[s], upd)
            iupd = jnp.where(at & jnp.logical_not(below), mult[s], iupd)
        a_ref[...] = jnp.where(below, upd, whole)
        inv_ref[...] = iupd
        a_ref[pl.ds(c0, b), :] = row
        inv_ref[pl.ds(c0, b), :] = jnp.where(lanes8 < c0 + subl, irow, inv_ref[pl.ds(c0, b), :])
        return carry

    lax.fori_loop(0, n // b, block, 0)


def exchange_kernel(
    pivots, mat, held, fix,
    panel, contrib, xbuf, dbuf, moved, diag, low_rows, inv, packed, solved, right_upper, right_rows, src_v, src_s, piv_v, piv_s,
    pivot_sem, load_sem, piece_sem, src_sem, recv_sem, tree_sem, part_sem, x_send, x_recv, d_send, d_recv,
    z_send, y_send, f_recv, c_send, c_recv, low_tree, low_part, low_recv,
):
    rows_local = held.shape[0]
    share = rows_local // TREES
    chunks = share // CHUNK
    per_piece = chunks // PIECES
    piece_rows = per_piece * CHUNK
    px = lax.axis_index("prow")
    pc = lax.axis_index("pcol")
    core = lax.rem(pc, 2)
    chip = lax.div(pc, 2)
    y = lax.div(chip, SIDE)
    z = lax.rem(chip, SIDE)
    is_root = pc == 0
    is_root1 = pc == 1
    partner = (px, pc + 1 - 2 * core)

    def pcol_of(yy, zz):
        return (lax.rem(yy + SIDE, SIDE) * SIDE + lax.rem(zz + SIDE, SIDE)) * 2 + core

    x_peers = [(lax.rem(px + k, SIDE), pc) for k in range(1, SIDE)]
    y_peers = [(px, pcol_of(y + k, z)) for k in range(1, SIDE)]
    z_peers = [(px, pcol_of(y, z + k)) for k in range(1, SIDE)]
    cross = [(lax.rem(px + k, SIDE), 1 - pc) for k in range(1, SIDE)]

    def remote(src, dst, send, recv, where):
        return pltpu.make_async_remote_copy(
            src_ref=src, dst_ref=dst, send_sem=send, recv_sem=recv, device_id=where, device_id_type=MESH
        )

    pivot_copies = [
        pltpu.make_async_copy(pivots, piv_s, pivot_sem.at[0]),
        pltpu.make_async_copy(pivots, piv_v, pivot_sem.at[1]),
    ]
    for copy in pivot_copies:
        copy.start()

    hold = pltpu.make_async_copy(mat, held, load_sem)
    pieces = []
    for q in range(PIECES):
        for t in range(TREES):
            part = pl.ds(t * share + q * piece_rows, piece_rows)
            pieces.append(pltpu.make_async_copy(mat.at[part], panel.at[part], piece_sem.at[q * TREES + t]))

    @pl.when(is_root)
    def _():
        for piece in pieces:
            piece.start()

    @pl.when(jnp.logical_not(is_root))
    def _():
        hold.start()

    barrier = pltpu.get_barrier_semaphore()
    for where in x_peers + y_peers + z_peers + [partner]:
        pl.semaphore_signal(barrier, inc=1, device_id=where, device_id_type=MESH)

    @pl.when(pc < 2)
    def _():
        for where in cross:
            pl.semaphore_signal(barrier, inc=1, device_id=where, device_id_type=MESH)

    to_scalars = pltpu.make_async_copy(src_v, src_s, src_sem)

    def find_sources():
        for copy in pivot_copies:
            copy.wait()
        which = lax.broadcasted_iota(jnp.int32, (8, NB), 0)
        sources = jnp.where(which == 0, lax.broadcasted_iota(jnp.int32, (8, NB), 1), piv_v[...])

        def back(step, sources):
            column = NB - 1 - step
            other = piv_s[0, column]
            return jnp.where(sources == column, other, jnp.where(sources == other, column, sources))

        src_v[...] = lax.fori_loop(0, NB, back, sources, unroll=8)
        to_scalars.start()

    @pl.when(jnp.logical_not(is_root))
    def _():
        find_sources()

    @pl.when(pc < 2)
    def _():
        pl.semaphore_wait(barrier, 13)

    @pl.when(pc >= 2)
    def _():
        pl.semaphore_wait(barrier, 10)

    feeds, delay = [], []
    targets = [(px, pcol_of(y + dy, z + dz)) for dy, dz in STEPS]
    for t in range(TREES):
        feeds.append([one_of(chip, SENDERS[t][d]) for d in range(4)])
        late = 0
        for place, lag in enumerate(lags(t)):
            late = late + jnp.where(chip == place, lag, 0)
        delay.append(late)

    def chunk_at(t, c):
        return panel.at[pl.ds(pl.multiple_of(t * share + c * CHUNK, CHUNK), CHUNK)]

    def forward(t, c):
        block = chunk_at(t, c)
        arrival = recv_sem.at[t * chunks + c]
        for d in range(4):

            @pl.when(feeds[t][d])
            def _():
                remote(block, block, tree_sem.at[t * 4 + d], arrival, targets[d]).start()

        remote(block, block, part_sem.at[t], arrival, partner).start()

    def low_piece(t):
        return low_rows.at[pl.ds(t * (NB // TREES), NB // TREES)]

    def forward_low(t):
        low = low_piece(t)
        for d in range(4):

            @pl.when(feeds[t][d])
            def _():
                remote(low, low, low_tree.at[t * 4 + d], low_recv.at[t], targets[d]).start()

        remote(low, low, low_part.at[t], low_recv.at[t], partner).start()

    def forward_range(lo, hi):
        def one(c, carry):
            for t in range(TREES):
                forward(t, c)
            return carry

        lax.fori_loop(lo, hi, one, 0)

    @pl.when(is_root)
    def _():
        for piece in pieces[:TREES]:
            piece.wait()
        forward_range(0, per_piece)
        find_sources()


    def gather(g, rows_ref):
        for r in range(2):
            base = pl.multiple_of(g * 8, 8)
            found = []
            for s in range(8):
                source = src_s[r, g * 8 + s]
                block = lax.div(source, NB)
                mine = lax.rem(block, SIDE) == px
                local = lax.div(block, SIDE) * NB + lax.rem(source, NB)
                row = rows_ref[pl.ds(jnp.where(mine, local, 0), 1), :]
                found.append(jnp.where(mine, row, 0.0))
            contrib[pl.ds(r * NB + base, 8), :] = jnp.concatenate(found, axis=0)

    def gather_from(rows_ref):
        def one(g, carry):
            gather(g, rows_ref)
            return carry

        lax.fori_loop(0, NB // 8, one, 0)

    @pl.when(is_root)
    def _():
        for piece in pieces[TREES:]:
            piece.wait()
        to_scalars.wait()
        gather_from(panel)

    @pl.when(core == 1)
    def _():
        to_scalars.wait()
        hold.wait()
        gather_from(held)

    d_copies = []
    for k in range(SIDE):
        where = (lax.rem(px + k, SIDE), pc + 1)
        d_copies.append(remote(contrib.at[pl.ds(0, NB)], dbuf.at[px], d_send.at[k], d_recv.at[px], where))

    @pl.when(is_root)
    def _():
        for copy in d_copies:
            copy.start()

    x_copies = [
        remote(contrib, xbuf.at[px], x_send.at[k], x_recv.at[px], x_peers[k]) for k in range(SIDE - 1)
    ]

    @pl.when(jnp.logical_or(core == 1, is_root))
    def _():
        for copy in x_copies:
            copy.start()

    def arrived(ref, sem):
        pltpu.make_async_copy(ref, ref, sem).wait()

    def receive_moved():
        total = contrib[...]
        for k in range(1, SIDE):
            slot = lax.rem(px + k, SIDE)
            arrived(xbuf.at[slot], x_recv.at[slot])
            total = total + xbuf[slot]
        moved[...] = total

    def solve_rows():
        solved[...] = factors(inv[...], moved[pl.ds(0, NB), :])[1]

    def split_factors():
        upper = factors(inv[...], moved[pl.ds(0, NB), :])[0]
        right_upper[...] = right_side(upper)
        right_rows[...] = right_side(solved[...])

    def take_factors():
        solve_rows()
        split_factors()

    def make_fix():
        low = product(low_rows[...], right_upper[...])
        fix[...] = jnp.where(is_root, low, moved[pl.ds(NB, NB), :] - product(low, right_rows[...]))

    def update(starts, size):
        places = [pl.ds(pl.multiple_of(start, CHUNK), size) for start in starts]
        old = [held[place, :] for place in places]
        upper, rows = right_upper[...], right_rows[...]
        lows = [product(panel[place, :], upper) for place in places]
        for place, x, low in zip(places, old, lows):
            held[place, :] = jnp.where(is_root, low, x - product(low, rows))

    def update_group(g, width):
        update([t * share + g * CHUNK for t in range(TREES)], width * CHUNK)

    def update_rest(lo, hi):
        def one(m, carry):
            update_group(m * WIDE, WIDE)
            return carry

        lax.fori_loop(lax.div(lo, WIDE), hi // WIDE, one, 0)

    @pl.when(is_root)
    def _():
        low_at = min(LOW_AT, chunks - 1)
        forward_range(per_piece, low_at)
        receive_moved()
        low_rows[...] = moved[pl.ds(NB, NB), :]
        for t in range(TREES):
            forward_low(t)
        forward_range(low_at, chunks)
        arrived(packed, c_recv.at[0])
        arrived(inv, c_recv.at[1])
        take_factors()
        make_fix()
        update_rest(jnp.int32(0), chunks)

    assert (FASTER - READY) % WIDE == 0 and READY >= max(max(lags(t)) for t in range(TREES))
    slow = min(FASTER - READY, chunks)
    last = functools.reduce(jnp.maximum, delay) + chunks
    pairs = lax.div(jnp.clip(last - FASTER, 0, (chunks - slow) // 2) + 1, 2) * 2
    done = slow + 2 * pairs

    @pl.when(jnp.logical_and(core == 0, jnp.logical_not(is_root)))
    def _():
        def relay(i, carry):
            for t in range(TREES):
                c = i - delay[t]

                @pl.when(c == min(LOW_AT, chunks - 1))
                def _():
                    arrived(low_piece(t), low_recv.at[t])
                    forward_low(t)

                @pl.when(jnp.logical_and(c >= 0, c < chunks))
                def _():
                    arrived(chunk_at(t, c), recv_sem.at[t * chunks + c])
                    forward(t, c)

            return carry

        def relay_and_one(i, carry):
            relay(i, carry)
            update_group(i - READY, 1)
            return carry

        def relay_and_two(i, carry):
            relay(i, carry)
            update_group(slow + (i - FASTER) * 2, 2)
            return carry

        def relay_and_gather(i, carry):
            relay(i, carry)
            gather(i - first, held)
            return carry

        first = PLAIN + 1
        lax.fori_loop(0, first, relay, 0)
        to_scalars.wait()
        hold.wait()
        lax.fori_loop(first, first + NB // 8, relay_and_gather, 0)
        for copy in x_copies:
            copy.start()
        lax.fori_loop(first + NB // 8, EARLY, relay, 0)
        receive_moved()
        lax.fori_loop(EARLY, READY - 1, relay, 0)
        arrived(packed, c_recv.at[0])
        arrived(inv, c_recv.at[1])
        solve_rows()
        lax.fori_loop(READY - 1, READY, relay, 0)
        split_factors()
        lax.fori_loop(READY, FASTER, relay_and_one, 0)
        make_fix()
        lax.fori_loop(FASTER, FASTER + pairs, relay_and_two, 0)
        update_rest(done, chunks)

    z_copies = [remote(diag, diag, z_send.at[k], f_recv, z_peers[k]) for k in range(3)]
    y_copies = [remote(diag, diag, y_send.at[k], f_recv, y_peers[k]) for k in range(3)]
    c_copies = [
        remote(packed, packed, c_send.at[0], c_recv.at[0], partner),
        remote(inv, inv, c_send.at[1], c_recv.at[1], partner),
    ]

    @pl.when(core == 1)
    def _():
        @pl.when(is_root1)
        def _():
            for k in range(SIDE):
                arrived(dbuf.at[k], d_recv.at[k])
            diag[...] = dbuf[0] + dbuf[1] + dbuf[2] + dbuf[3]
            for k in range(3):
                z_copies[k].start()
            for k in range(3):
                y_copies[k].start()

        @pl.when(jnp.logical_not(is_root1))
        def _():
            arrived(diag, f_recv)

            @pl.when(y == 0)
            def _():
                for k in range(3):
                    y_copies[k].start()

        packed[...] = diag[...]
        eliminate_and_invert(packed, inv)
        c_copies[1].start()
        c_copies[0].start()
        receive_moved()
        take_factors()

        def receive(m, carry):
            for i in (2 * m, 2 * m + 1):
                for t in range(TREES):
                    arrived(chunk_at(t, i), recv_sem.at[t * chunks + i])
            update_group(2 * m, 2)
            return carry

        late = chunks // 2 - chunks // 8
        lax.fori_loop(0, late, receive, 0)
        for t in range(TREES):
            arrived(low_piece(t), low_recv.at[t])
        make_fix()
        def receive_one(i, carry):
            for t in range(TREES):
                arrived(chunk_at(t, i), recv_sem.at[t * chunks + i])
            update_group(i, 1)
            return carry

        lax.fori_loop(late, chunks // 2 - 1, receive, 0)
        lax.fori_loop(chunks - 2, chunks, receive_one, 0)

        for copy in c_copies:
            copy.wait_send()

        @pl.when(is_root1)
        def _():
            for copy in z_copies:
                copy.wait_send()

        @pl.when(y == 0)
        def _():
            for copy in y_copies:
                copy.wait_send()

    @pl.when(core == 0)
    def _():
        for t in range(TREES):
            sent = panel.at[pl.ds(t * share, share)]
            for d in range(4):

                @pl.when(feeds[t][d])
                def _():
                    remote(sent, sent, tree_sem.at[t * 4 + d], recv_sem.at[0], partner).wait_send()

            remote(sent, sent, part_sem.at[t], recv_sem.at[0], partner).wait_send()
            low = low_piece(t)
            for d in range(4):

                @pl.when(feeds[t][d])
                def _():
                    remote(low, low, low_tree.at[t * 4 + d], low_recv.at[t], partner).wait_send()

            remote(low, low, low_part.at[t], low_recv.at[t], partner).wait_send()

        @pl.when(is_root)
        def _():
            for copy in d_copies:
                copy.wait_send()

    @pl.when(px == 0)
    def _():
        held[pl.ds(0, NB), :] = jnp.where(is_root, packed[...], solved[...])

    for copy in x_copies:
        copy.wait_send()


def split(x):
    high = x.astype(BF16)
    return high, (x - high.astype(F32)).astype(BF16)


def right_side(x):
    high, low = split(x)
    return jnp.concatenate(
        [jnp.concatenate([high, low], axis=1), jnp.concatenate([high, jnp.zeros_like(low)], axis=1)], axis=0
    )


def product(x, right):
    high, low = split(x)
    both = jnp.dot(jnp.concatenate([high, low], axis=1), right, preferred_element_type=F32)
    return both[:, :NB] + both[:, NB:]


def factors(inv, moved_top):
    rows = lax.broadcasted_iota(jnp.int32, (NB, NB), 0)
    lanes = lax.broadcasted_iota(jnp.int32, (NB, NB), 1)
    upper = jnp.where(rows <= lanes, inv, 0.0)
    lower = jnp.where(rows > lanes, inv, jnp.where(rows == lanes, 1.0, 0.0))
    urows = jnp.dot(lower, moved_top, precision=lax.Precision.HIGHEST, preferred_element_type=F32)
    return upper, urows


def finish_kernel(piv_s, held, fix, out, rows_s, store_sem, row_sem):
    blocks = store_sem.shape[0]
    size = held.shape[0] // blocks
    px = lax.axis_index("prow")
    stores = []
    for b in range(blocks):
        part = pl.ds(b * size, size)
        stores.append(pltpu.make_async_copy(held.at[part], out.at[part], store_sem.at[b]))
    for store in stores:
        store.start()

    def note(j, count):
        target = piv_s[j]
        place = lax.div(target, NB)
        mine = jnp.logical_and(lax.rem(place, SIDE) == px, place > 0)
        rows_s[0, count] = lax.div(place, SIDE) * NB + lax.rem(target, NB)
        rows_s[1, count] = j
        return count + jnp.where(mine, 1, 0)

    count = lax.fori_loop(0, NB, note, jnp.int32(0), unroll=8)
    for store in stores:
        store.wait()

    def row_copy(i):
        here, there = rows_s[1, i], rows_s[0, i]
        return pltpu.make_async_copy(fix.at[pl.ds(here, 1)], out.at[pl.ds(there, 1)], row_sem)

    def start(i, carry):
        row_copy(i).start()
        return carry

    def finish(i, carry):
        row_copy(0).wait()
        return carry

    lax.fori_loop(0, count, start, 0)
    lax.fori_loop(0, count, finish, 0)


def local(matrix, pivots):
    rows_local = matrix.shape[0] * matrix.shape[2]
    held = matrix.reshape(rows_local, NB)
    chunks = rows_local // CHUNK
    smem = pl.BlockSpec(memory_space=pltpu.SMEM)
    vmem = pl.BlockSpec(memory_space=pltpu.VMEM)
    hbm = pl.BlockSpec(memory_space=pl.ANY)
    square = pltpu.VMEM((NB, NB), F32)
    dma = pltpu.SemaphoreType.DMA
    changed, fix = pl.pallas_call(
        exchange_kernel,
        out_shape=(
            jax.ShapeDtypeStruct((rows_local, NB), F32),
            jax.ShapeDtypeStruct((NB, NB), F32),
        ),
        in_specs=[pl.BlockSpec(memory_space=pltpu.HBM), hbm],
        out_specs=(vmem,) * 2,
        scratch_shapes=[
            pltpu.VMEM((rows_local, NB), F32),
            pltpu.VMEM((2 * NB, NB), F32),
            pltpu.VMEM((SIDE, 2 * NB, NB), F32),
            pltpu.VMEM((SIDE, NB, NB), F32),
            pltpu.VMEM((2 * NB, NB), F32),
            square,
            square,
            square,
            square,
            square,
            pltpu.VMEM((2 * NB, 2 * NB), BF16),
            pltpu.VMEM((2 * NB, 2 * NB), BF16),
            pltpu.VMEM((8, NB), jnp.int32),
            pltpu.SMEM((8, NB), jnp.int32),
            pltpu.VMEM((1, NB), jnp.int32),
            pltpu.SMEM((1, NB), jnp.int32),
            dma((2,)),
            dma,
            dma((PIECES * TREES,)),
            dma,
            dma((chunks,)),
            dma((TREES * 4,)),
            dma((TREES,)),
            dma((SIDE - 1,)),
            dma((SIDE,)),
            dma((SIDE,)),
            dma((SIDE,)),
            dma((3,)),
            dma((3,)),
            dma,
            dma((2,)),
            dma((2,)),
            dma((TREES * 4,)),
            dma((TREES,)),
            dma((TREES,)),
        ],
        compiler_params=pltpu.CompilerParams(
            collective_id=0, has_side_effects=True, vmem_limit_bytes=VMEM_MIB * 2**20
        ),
    )(pltpu.with_memory_space_constraint(pivots.reshape(1, NB), pltpu.HBM), held)
    out = pl.pallas_call(
        finish_kernel,
        out_shape=jax.ShapeDtypeStruct((rows_local, NB), F32),
        in_specs=[smem, vmem, vmem],
        out_specs=hbm,
        scratch_shapes=[pltpu.SMEM((2, 2 * NB), jnp.int32), dma((4,)), dma],
        compiler_params=pltpu.CompilerParams(vmem_limit_bytes=4 * 2**20),
    )(pivots, changed, fix)
    return out.reshape(matrix.shape)


def solution(mesh):
    return jax.shard_map(
        local,
        mesh=mesh,
        in_specs=(P(None, "prow", None, None, "pcol", None), P()),
        out_specs=P(None, "prow", None, None, "pcol", None),
        check_vma=False,
    )
```

```python
import functools

import jax
import jax.numpy as jnp
from jax import lax
from jax.experimental import pallas as pl
from jax.experimental.pallas import tpu as pltpu
from jax.sharding import PartitionSpec as P

MESH = pl.DeviceIdType.MESH
F32 = jnp.float32
BF16 = jnp.bfloat16
NB = 128
SIDE = 4
TREES = 4
STEPS = ((1, 0), (-1, 0), (0, 1), (0, -1))
SENDERS = (
    ((0, 4, 8, 9, 10, 11), (5, 6, 7), (4, 5, 8, 9), (4, 8)),
    ((13, 14, 15), (0, 8, 9, 10, 11, 12, 13, 14, 15), (12, 13), (12,)),
    ((1, 2, 5, 6), (1, 2), (0, 1, 2, 6, 10, 14), (5, 9, 13)),
    ((3, 7), (3,), (7, 11, 15), (0, 2, 3, 6, 7, 10, 11, 14, 15)),
)
PLAIN, ROUND = 5, 6
CHUNK = 128
PIECES = 4
EARLY = 32
LOW_AT = 20
READY = 39
FASTER = 51
WIDE = 4
VMEM_MIB = 40


def one_of(value, places):
    found = value < 0
    for place in places:
        found = jnp.logical_or(found, value == place)
    return found


def lags(tree):
    lag = {0: 0}
    while len(lag) < SIDE * SIDE:
        for d, places in enumerate(SENDERS[tree]):
            for place in places:
                if place in lag:
                    y, z = place // SIDE + STEPS[d][0], place % SIDE + STEPS[d][1]
                    plain = 0 <= y < SIDE and 0 <= z < SIDE
                    lag[y % SIDE * SIDE + z % SIDE] = lag[place] + (PLAIN if plain else ROUND)
    return [lag[place] for place in range(SIDE * SIDE)]


def eliminate_and_invert(a_ref, inv_ref):
    n, b = NB, 8
    lanes1 = lax.broadcasted_iota(jnp.int32, (1, n), 1)
    lanes8 = lax.broadcasted_iota(jnp.int32, (b, n), 1)
    subl = lax.broadcasted_iota(jnp.int32, (b, n), 0)
    rows = lax.broadcasted_iota(jnp.int32, (n, n), 0)
    lanes = lax.broadcasted_iota(jnp.int32, (n, n), 1)
    inv_ref[...] = jnp.zeros((n, n), F32)

    def block(k, carry):
        c0 = pl.multiple_of(k * b, b)

        def pick(x, j):
            return jnp.take_along_axis(x, jnp.full(x.shape, c0 + j, jnp.int32), axis=1)

        row = a_ref[pl.ds(c0, b), :]
        irow = inv_ref[pl.ds(c0, b), :]
        cols = [pick(row, j) for j in range(b)]
        recs, us, prow, pinv, gs = [], {}, [], [], []
        for s in range(b):
            r = 1.0 / jnp.broadcast_to(cols[s][s : s + 1], (b, n))
            recs.append(r[0:1])
            g = jnp.where(subl > s, cols[s] * r, 0.0)
            gs.append(g)
            for j in range(s + 1, b):
                us[s, j] = cols[j][s : s + 1]
                cols[j] = cols[j] - g * us[s, j]
            ar = jnp.where(lanes1 > c0 + s, row[s : s + 1], 0.0)
            row = row - g * ar
            ir = jnp.where(lanes1 == c0 + s, 1.0, irow[s : s + 1])
            irow = irow - g * ir
            prow.append(ar)
            pinv.append(ir)
        for s in range(b):
            row = jnp.where((lanes8 == c0 + s) & (subl > s), gs[s], row)
        whole = a_ref[...]
        inverse = inv_ref[...]
        below = rows >= c0 + b
        own = jnp.where(rows == lanes, 1.0, 0.0)
        mix = jnp.where(below, whole, jnp.where(rows < c0, inverse, own))
        mult = []
        for j in range(b):
            c = pick(mix, j)
            for s in range(j):
                c = c - mult[s] * us[s, j]
            mult.append(c * recs[j])
        upd = whole
        iupd = jnp.where((rows >= c0) & (rows < c0 + b), 0.0, inverse)
        for s in range(b):
            upd = upd - mult[s] * prow[s]
            iupd = iupd - mult[s] * jnp.where(below, pinv[s], prow[s])
        for s in range(b):
            at = lanes == c0 + s
            upd = jnp.where(at, mult[s], upd)
            iupd = jnp.where(at & jnp.logical_not(below), mult[s], iupd)
        a_ref[...] = jnp.where(below, upd, whole)
        inv_ref[...] = iupd
        a_ref[pl.ds(c0, b), :] = row
        inv_ref[pl.ds(c0, b), :] = jnp.where(lanes8 < c0 + subl, irow, inv_ref[pl.ds(c0, b), :])
        return carry

    lax.fori_loop(0, n // b, block, 0)


def exchange_kernel(
    pivots, mat, held, fix,
    panel, contrib, xbuf, dbuf, moved, diag, low_rows, inv, packed, solved, right_upper, right_rows, src_v, src_s, piv_v, piv_s,
    pivot_sem, load_sem, piece_sem, src_sem, recv_sem, tree_sem, part_sem, x_send, x_recv, d_send, d_recv,
    z_send, y_send, f_recv, c_send, c_recv, low_tree, low_part, low_recv,
):
    rows_local = held.shape[0]
    share = rows_local // TREES
    chunks = share // CHUNK
    per_piece = chunks // PIECES
    piece_rows = per_piece * CHUNK
    px = lax.axis_index("prow")
    pc = lax.axis_index("pcol")
    core = lax.rem(pc, 2)
    chip = lax.div(pc, 2)
    y = lax.div(chip, SIDE)
    z = lax.rem(chip, SIDE)
    is_root = pc == 0
    is_root1 = pc == 1
    partner = (px, pc + 1 - 2 * core)

    def pcol_of(yy, zz):
        return (lax.rem(yy + SIDE, SIDE) * SIDE + lax.rem(zz + SIDE, SIDE)) * 2 + core

    x_peers = [(lax.rem(px + k, SIDE), pc) for k in range(1, SIDE)]
    y_peers = [(px, pcol_of(y + k, z)) for k in range(1, SIDE)]
    z_peers = [(px, pcol_of(y, z + k)) for k in range(1, SIDE)]
    cross = [(lax.rem(px + k, SIDE), 1 - pc) for k in range(1, SIDE)]

    def remote(src, dst, send, recv, where):
        return pltpu.make_async_remote_copy(
            src_ref=src, dst_ref=dst, send_sem=send, recv_sem=recv, device_id=where, device_id_type=MESH
        )

    pivot_copies = [
        pltpu.make_async_copy(pivots, piv_s, pivot_sem.at[0]),
        pltpu.make_async_copy(pivots, piv_v, pivot_sem.at[1]),
    ]
    for copy in pivot_copies:
        copy.start()

    hold = pltpu.make_async_copy(mat, held, load_sem)
    pieces = []
    for q in range(PIECES):
        for t in range(TREES):
            part = pl.ds(t * share + q * piece_rows, piece_rows)
            pieces.append(pltpu.make_async_copy(mat.at[part], panel.at[part], piece_sem.at[q * TREES + t]))

    @pl.when(is_root)
    def _():
        for piece in pieces:
            piece.start()

    @pl.when(jnp.logical_not(is_root))
    def _():
        hold.start()

    barrier = pltpu.get_barrier_semaphore()
    for where in x_peers + y_peers + z_peers + [partner]:
        pl.semaphore_signal(barrier, inc=1, device_id=where, device_id_type=MESH)

    @pl.when(pc < 2)
    def _():
        for where in cross:
            pl.semaphore_signal(barrier, inc=1, device_id=where, device_id_type=MESH)

    to_scalars = pltpu.make_async_copy(src_v, src_s, src_sem)

    def find_sources():
        for copy in pivot_copies:
            copy.wait()
        which = lax.broadcasted_iota(jnp.int32, (8, NB), 0)
        sources = jnp.where(which == 0, lax.broadcasted_iota(jnp.int32, (8, NB), 1), piv_v[...])

        def back(step, sources):
            column = NB - 1 - step
            other = piv_s[0, column]
            return jnp.where(sources == column, other, jnp.where(sources == other, column, sources))

        src_v[...] = lax.fori_loop(0, NB, back, sources, unroll=8)
        to_scalars.start()

    @pl.when(jnp.logical_not(is_root))
    def _():
        find_sources()

    @pl.when(pc < 2)
    def _():
        pl.semaphore_wait(barrier, 13)

    @pl.when(pc >= 2)
    def _():
        pl.semaphore_wait(barrier, 10)

    feeds, delay = [], []
    targets = [(px, pcol_of(y + dy, z + dz)) for dy, dz in STEPS]
    for t in range(TREES):
        feeds.append([one_of(chip, SENDERS[t][d]) for d in range(4)])
        late = 0
        for place, lag in enumerate(lags(t)):
            late = late + jnp.where(chip == place, lag, 0)
        delay.append(late)

    def chunk_at(t, c):
        return panel.at[pl.ds(pl.multiple_of(t * share + c * CHUNK, CHUNK), CHUNK)]

    def forward(t, c):
        block = chunk_at(t, c)
        arrival = recv_sem.at[t * chunks + c]
        for d in range(4):

            @pl.when(feeds[t][d])
            def _():
                remote(block, block, tree_sem.at[t * 4 + d], arrival, targets[d]).start()

        remote(block, block, part_sem.at[t], arrival, partner).start()

    def low_piece(t):
        return low_rows.at[pl.ds(t * (NB // TREES), NB // TREES)]

    def forward_low(t):
        low = low_piece(t)
        for d in range(4):

            @pl.when(feeds[t][d])
            def _():
                remote(low, low, low_tree.at[t * 4 + d], low_recv.at[t], targets[d]).start()

        remote(low, low, low_part.at[t], low_recv.at[t], partner).start()

    def forward_range(lo, hi):
        def one(c, carry):
            for t in range(TREES):
                forward(t, c)
            return carry

        lax.fori_loop(lo, hi, one, 0)

    @pl.when(is_root)
    def _():
        for piece in pieces[:TREES]:
            piece.wait()
        forward_range(0, per_piece)
        find_sources()


    def gather(g, rows_ref):
        for r in range(2):
            base = pl.multiple_of(g * 8, 8)
            found = []
            for s in range(8):
                source = src_s[r, g * 8 + s]
                block = lax.div(source, NB)
                mine = lax.rem(block, SIDE) == px
                local = lax.div(block, SIDE) * NB + lax.rem(source, NB)
                row = rows_ref[pl.ds(jnp.where(mine, local, 0), 1), :]
                found.append(jnp.where(mine, row, 0.0))
            contrib[pl.ds(r * NB + base, 8), :] = jnp.concatenate(found, axis=0)

    def gather_from(rows_ref):
        def one(g, carry):
            gather(g, rows_ref)
            return carry

        lax.fori_loop(0, NB // 8, one, 0)

    @pl.when(is_root)
    def _():
        for piece in pieces[TREES:]:
            piece.wait()
        to_scalars.wait()
        gather_from(panel)

    @pl.when(core == 1)
    def _():
        to_scalars.wait()
        hold.wait()
        gather_from(held)

    d_copies = []
    for k in range(SIDE):
        where = (lax.rem(px + k, SIDE), pc + 1)
        d_copies.append(remote(contrib.at[pl.ds(0, NB)], dbuf.at[px], d_send.at[k], d_recv.at[px], where))

    @pl.when(is_root)
    def _():
        for copy in d_copies:
            copy.start()

    x_copies = [
        remote(contrib, xbuf.at[px], x_send.at[k], x_recv.at[px], x_peers[k]) for k in range(SIDE - 1)
    ]

    @pl.when(jnp.logical_or(core == 1, is_root))
    def _():
        for copy in x_copies:
            copy.start()

    def arrived(ref, sem):
        pltpu.make_async_copy(ref, ref, sem).wait()

    def receive_moved():
        total = contrib[...]
        for k in range(1, SIDE):
            slot = lax.rem(px + k, SIDE)
            arrived(xbuf.at[slot], x_recv.at[slot])
            total = total + xbuf[slot]
        moved[...] = total

    def solve_rows():
        solved[...] = factors(inv[...], moved[pl.ds(0, NB), :])[1]

    def split_factors():
        upper = factors(inv[...], moved[pl.ds(0, NB), :])[0]
        right_upper[...] = right_side(upper)
        right_rows[...] = right_side(solved[...])

    def take_factors():
        solve_rows()
        split_factors()

    def make_fix():
        low = product(low_rows[...], right_upper[...])
        fix[...] = jnp.where(is_root, low, moved[pl.ds(NB, NB), :] - product(low, right_rows[...]))

    def update(starts, size):
        places = [pl.ds(pl.multiple_of(start, CHUNK), size) for start in starts]
        old = [held[place, :] for place in places]
        upper, rows = right_upper[...], right_rows[...]
        lows = [product(panel[place, :], upper) for place in places]
        for place, x, low in zip(places, old, lows):
            held[place, :] = jnp.where(is_root, low, x - product(low, rows))

    def update_group(g, width):
        update([t * share + g * CHUNK for t in range(TREES)], width * CHUNK)

    def update_rest(lo, hi):
        def one(m, carry):
            update_group(m * WIDE, WIDE)
            return carry

        lax.fori_loop(lax.div(lo, WIDE), hi // WIDE, one, 0)

    @pl.when(is_root)
    def _():
        low_at = min(LOW_AT, chunks - 1)
        forward_range(per_piece, low_at)
        receive_moved()
        low_rows[...] = moved[pl.ds(NB, NB), :]
        for t in range(TREES):
            forward_low(t)
        forward_range(low_at, chunks)
        arrived(packed, c_recv.at[0])
        arrived(inv, c_recv.at[1])
        take_factors()
        make_fix()
        update_rest(jnp.int32(0), chunks)

    assert (FASTER - READY) % WIDE == 0 and READY >= max(max(lags(t)) for t in range(TREES))
    slow = min(FASTER - READY, chunks)
    last = functools.reduce(jnp.maximum, delay) + chunks
    pairs = lax.div(jnp.clip(last - FASTER, 0, (chunks - slow) // 2) + 1, 2) * 2
    done = slow + 2 * pairs

    @pl.when(jnp.logical_and(core == 0, jnp.logical_not(is_root)))
    def _():
        def relay(i, carry):
            for t in range(TREES):
                c = i - delay[t]

                @pl.when(c == min(LOW_AT, chunks - 1))
                def _():
                    arrived(low_piece(t), low_recv.at[t])
                    forward_low(t)

                @pl.when(jnp.logical_and(c >= 0, c < chunks))
                def _():
                    arrived(chunk_at(t, c), recv_sem.at[t * chunks + c])
                    forward(t, c)

            return carry

        def relay_and_one(i, carry):
            relay(i, carry)
            update_group(i - READY, 1)
            return carry

        def relay_and_two(i, carry):
            relay(i, carry)
            update_group(slow + (i - FASTER) * 2, 2)
            return carry

        def relay_and_gather(i, carry):
            relay(i, carry)
            gather(i - first, held)
            return carry

        first = PLAIN + 1
        lax.fori_loop(0, first, relay, 0)
        to_scalars.wait()
        hold.wait()
        lax.fori_loop(first, first + NB // 8, relay_and_gather, 0)
        for copy in x_copies:
            copy.start()
        lax.fori_loop(first + NB // 8, EARLY, relay, 0)
        receive_moved()
        lax.fori_loop(EARLY, READY - 1, relay, 0)
        arrived(packed, c_recv.at[0])
        arrived(inv, c_recv.at[1])
        solve_rows()
        lax.fori_loop(READY - 1, READY, relay, 0)
        split_factors()
        lax.fori_loop(READY, FASTER, relay_and_one, 0)
        make_fix()
        lax.fori_loop(FASTER, FASTER + pairs, relay_and_two, 0)
        update_rest(done, chunks)

    z_copies = [remote(diag, diag, z_send.at[k], f_recv, z_peers[k]) for k in range(3)]
    y_copies = [remote(diag, diag, y_send.at[k], f_recv, y_peers[k]) for k in range(3)]
    c_copies = [
        remote(packed, packed, c_send.at[0], c_recv.at[0], partner),
        remote(inv, inv, c_send.at[1], c_recv.at[1], partner),
    ]

    @pl.when(core == 1)
    def _():
        @pl.when(is_root1)
        def _():
            for k in range(SIDE):
                arrived(dbuf.at[k], d_recv.at[k])
            diag[...] = dbuf[0] + dbuf[1] + dbuf[2] + dbuf[3]
            for k in range(3):
                z_copies[k].start()
            for k in range(3):
                y_copies[k].start()

        @pl.when(jnp.logical_not(is_root1))
        def _():
            arrived(diag, f_recv)

            @pl.when(y == 0)
            def _():
                for k in range(3):
                    y_copies[k].start()

        packed[...] = diag[...]
        eliminate_and_invert(packed, inv)
        c_copies[1].start()
        c_copies[0].start()
        receive_moved()
        take_factors()

        def receive(m, carry):
            for i in (2 * m, 2 * m + 1):
                for t in range(TREES):
                    arrived(chunk_at(t, i), recv_sem.at[t * chunks + i])
            update_group(2 * m, 2)
            return carry

        late = chunks // 2 - chunks // 8
        lax.fori_loop(0, late, receive, 0)
        for t in range(TREES):
            arrived(low_piece(t), low_recv.at[t])
        make_fix()
        def receive_one(i, carry):
            for t in range(TREES):
                arrived(chunk_at(t, i), recv_sem.at[t * chunks + i])
            update_group(i, 1)
            return carry

        lax.fori_loop(late, chunks // 2 - 1, receive, 0)
        lax.fori_loop(chunks - 2, chunks, receive_one, 0)

        for copy in c_copies:
            copy.wait_send()

        @pl.when(is_root1)
        def _():
            for copy in z_copies:
                copy.wait_send()

        @pl.when(y == 0)
        def _():
            for copy in y_copies:
                copy.wait_send()

    @pl.when(core == 0)
    def _():
        for t in range(TREES):
            sent = panel.at[pl.ds(t * share, share)]
            for d in range(4):

                @pl.when(feeds[t][d])
                def _():
                    remote(sent, sent, tree_sem.at[t * 4 + d], recv_sem.at[0], partner).wait_send()

            remote(sent, sent, part_sem.at[t], recv_sem.at[0], partner).wait_send()
            low = low_piece(t)
            for d in range(4):

                @pl.when(feeds[t][d])
                def _():
                    remote(low, low, low_tree.at[t * 4 + d], low_recv.at[t], partner).wait_send()

            remote(low, low, low_part.at[t], low_recv.at[t], partner).wait_send()

        @pl.when(is_root)
        def _():
            for copy in d_copies:
                copy.wait_send()

    @pl.when(px == 0)
    def _():
        held[pl.ds(0, NB), :] = jnp.where(is_root, packed[...], solved[...])

    for copy in x_copies:
        copy.wait_send()


def split(x):
    high = x.astype(BF16)
    return high, (x - high.astype(F32)).astype(BF16)


def right_side(x):
    high, low = split(x)
    return jnp.concatenate(
        [jnp.concatenate([high, low], axis=1), jnp.concatenate([high, jnp.zeros_like(low)], axis=1)], axis=0
    )


def product(x, right):
    high, low = split(x)
    both = jnp.dot(jnp.concatenate([high, low], axis=1), right, preferred_element_type=F32)
    return both[:, :NB] + both[:, NB:]


def factors(inv, moved_top):
    rows = lax.broadcasted_iota(jnp.int32, (NB, NB), 0)
    lanes = lax.broadcasted_iota(jnp.int32, (NB, NB), 1)
    upper = jnp.where(rows <= lanes, inv, 0.0)
    lower = jnp.where(rows > lanes, inv, jnp.where(rows == lanes, 1.0, 0.0))
    urows = jnp.dot(lower, moved_top, precision=lax.Precision.HIGHEST, preferred_element_type=F32)
    return upper, urows


def finish_kernel(piv_s, held, fix, out, rows_s, store_sem, row_sem):
    blocks = store_sem.shape[0]
    size = held.shape[0] // blocks
    px = lax.axis_index("prow")
    stores = []
    for b in range(blocks):
        part = pl.ds(b * size, size)
        stores.append(pltpu.make_async_copy(held.at[part], out.at[part], store_sem.at[b]))
    for store in stores:
        store.start()

    def note(j, count):
        target = piv_s[j]
        place = lax.div(target, NB)
        mine = jnp.logical_and(lax.rem(place, SIDE) == px, place > 0)
        rows_s[0, count] = lax.div(place, SIDE) * NB + lax.rem(target, NB)
        rows_s[1, count] = j
        return count + jnp.where(mine, 1, 0)

    count = lax.fori_loop(0, NB, note, jnp.int32(0), unroll=8)
    for store in stores:
        store.wait()

    def row_copy(i):
        here, there = rows_s[1, i], rows_s[0, i]
        return pltpu.make_async_copy(fix.at[pl.ds(here, 1)], out.at[pl.ds(there, 1)], row_sem)

    def start(i, carry):
        row_copy(i).start()
        return carry

    def finish(i, carry):
        row_copy(0).wait()
        return carry

    lax.fori_loop(0, count, start, 0)
    lax.fori_loop(0, count, finish, 0)


def local(matrix, pivots):
    rows_local = matrix.shape[0] * matrix.shape[2]
    held = matrix.reshape(rows_local, NB)
    chunks = rows_local // CHUNK
    smem = pl.BlockSpec(memory_space=pltpu.SMEM)
    vmem = pl.BlockSpec(memory_space=pltpu.VMEM)
    hbm = pl.BlockSpec(memory_space=pl.ANY)
    square = pltpu.VMEM((NB, NB), F32)
    dma = pltpu.SemaphoreType.DMA
    changed, fix = pl.pallas_call(
        exchange_kernel,
        out_shape=(
            jax.ShapeDtypeStruct((rows_local, NB), F32),
            jax.ShapeDtypeStruct((NB, NB), F32),
        ),
        in_specs=[pl.BlockSpec(memory_space=pltpu.HBM), hbm],
        out_specs=(vmem,) * 2,
        scratch_shapes=[
            pltpu.VMEM((rows_local, NB), F32),
            pltpu.VMEM((2 * NB, NB), F32),
            pltpu.VMEM((SIDE, 2 * NB, NB), F32),
            pltpu.VMEM((SIDE, NB, NB), F32),
            pltpu.VMEM((2 * NB, NB), F32),
            square,
            square,
            square,
            square,
            square,
            pltpu.VMEM((2 * NB, 2 * NB), BF16),
            pltpu.VMEM((2 * NB, 2 * NB), BF16),
            pltpu.VMEM((8, NB), jnp.int32),
            pltpu.SMEM((8, NB), jnp.int32),
            pltpu.VMEM((1, NB), jnp.int32),
            pltpu.SMEM((1, NB), jnp.int32),
            dma((2,)),
            dma,
            dma((PIECES * TREES,)),
            dma,
            dma((chunks,)),
            dma((TREES * 4,)),
            dma((TREES,)),
            dma((SIDE - 1,)),
            dma((SIDE,)),
            dma((SIDE,)),
            dma((SIDE,)),
            dma((3,)),
            dma((3,)),
            dma,
            dma((2,)),
            dma((2,)),
            dma((TREES * 4,)),
            dma((TREES,)),
            dma((TREES,)),
        ],
        compiler_params=pltpu.CompilerParams(
            collective_id=0, has_side_effects=True, vmem_limit_bytes=VMEM_MIB * 2**20
        ),
    )(pltpu.with_memory_space_constraint(pivots.reshape(1, NB), pltpu.HBM), held)
    out = pl.pallas_call(
        finish_kernel,
        out_shape=jax.ShapeDtypeStruct((rows_local, NB), F32),
        in_specs=[smem, vmem, vmem],
        out_specs=hbm,
        scratch_shapes=[pltpu.SMEM((2, 2 * NB), jnp.int32), dma((4,)), dma],
        compiler_params=pltpu.CompilerParams(vmem_limit_bytes=4 * 2**20),
    )(pivots, changed, fix)
    return out.reshape(matrix.shape)


def solution(mesh):
    return jax.shard_map(
        local,
        mesh=mesh,
        in_specs=(P(None, "prow", None, None, "pcol", None), P()),
        out_specs=P(None, "prow", None, None, "pcol", None),
        check_vma=False,
    )
```
